32 devices in a mesh: ctx: 16 (over z, y, core), head: 2 (over x).
Axes of the slice: x: 2, y: 2, z: 4, core: 2. Of those that a mesh axis runs over, the one named last changes fastest.
Arguments:
- token_values: bfloat16 [8192, 8192], P('ctx', 'head'), may hold values from -6 to 6
- step_sizes: bfloat16 [128, 8192], P('head', 'ctx'), may hold values from 0 to 307.73287
- log_rates: float32 [128], P('head'), may hold values from -8 to 0
- state_write: bfloat16 [8192, 1024], P(('ctx', 'head')), may hold values from -0.53033009 to 0.53033009
- state_read: bfloat16 [8192, 1024], P(('ctx', 'head')), may hold values from -6 to 6
- skip_gain: float32 [128], P('head'), may hold values from 0.5 to 1.5
Outputs:
- mixer_out: bfloat16 [8192, 8192], P('ctx', 'head')
The draws below stay inside these ranges and needn't reach their ends.
All inputs are finite; a program needn't handle non-finite values.
Results may differ from the reference program's by a relative error of at most 0.006.
Values may be sent and summed in bfloat16 or wider, within the bound.
A program may use at most 192 MiB of HBM per device.

```python
import jax
import jax.numpy as jnp
from jax import lax

MIXER_HEADS = 128
HEAD_DIM = 64
STATE_SIZE = 128
SHARED_GROUPS = 8
SPAN = 256
TOK_DEV = 512
SEQUENCE_TOKENS = 8192


def spike_rows(key):
    return jax.random.randint(jax.random.fold_in(key, 11), (SHARED_GROUPS, SEQUENCE_TOKENS), 0, SEQUENCE_TOKENS) < 3


def head_law(key):
    choose = jax.random.uniform(jax.random.fold_in(key, 21), (MIXER_HEADS,))
    gentle_heads = choose < 0.5
    root_tokens = jnp.sqrt(jnp.float32(SEQUENCE_TOKENS))
    slow_rate = jnp.exp(jax.random.uniform(jax.random.fold_in(key, 22), (MIXER_HEADS,), minval=jnp.log(0.15), maxval=jnp.log(0.45))) / root_tokens
    fast_rate = jnp.exp(jax.random.uniform(jax.random.fold_in(key, 23), (MIXER_HEADS,), minval=jnp.log(0.15), maxval=jnp.log(0.3)))
    return (gentle_heads, jnp.where(gentle_heads, slow_rate, fast_rate))


def draw_log_rates(key, part):
    return jnp.log(head_law(key)[1]).astype(jnp.float32)


def draw_step_sizes(key, part):
    gentle_heads, head_rates = head_law(key)
    root_tokens = jnp.sqrt(jnp.float32(SEQUENCE_TOKENS))
    spike_flags = spike_rows(key)[jnp.arange(MIXER_HEADS) // (MIXER_HEADS // SHARED_GROUPS)]
    gentle_steps = jnp.exp(jax.random.uniform(jax.random.fold_in(key, 31), (MIXER_HEADS, SEQUENCE_TOKENS), minval=jnp.log(0.5), maxval=jnp.log(1.5))) / root_tokens
    quick_steps = jnp.exp(jax.random.uniform(jax.random.fold_in(key, 32), (MIXER_HEADS, SEQUENCE_TOKENS), minval=jnp.log(0.1), maxval=jnp.log(0.3)))
    decay_losses = jax.random.uniform(jax.random.fold_in(key, 33), (MIXER_HEADS, SEQUENCE_TOKENS), minval=0.22, maxval=0.5)
    spike_steps = decay_losses / head_rates[:, None]
    combined_steps = jnp.where(gentle_heads[:, None], jnp.where(spike_flags, spike_steps, gentle_steps), quick_steps)
    return combined_steps.astype(jnp.bfloat16)


def draw_state_write(key, part):
    spike_flags = jnp.repeat(spike_rows(key).T, STATE_SIZE, axis=1)
    normal_draw = jnp.clip(jax.random.normal(jax.random.fold_in(key, 41), (SEQUENCE_TOKENS, SHARED_GROUPS * STATE_SIZE)), -6.0, 6.0)
    scaled_sample = normal_draw / jnp.sqrt(jnp.float32(STATE_SIZE))
    return jnp.where(spike_flags, scaled_sample / jnp.float32(SEQUENCE_TOKENS), scaled_sample).astype(jnp.bfloat16)


def block_levels(stream_key, extent, pieces, least, top_value):
    def one(axis_at, shards_of):
        draws = jax.random.uniform(jax.random.fold_in(jax.random.fold_in(stream_key, 6), axis_at), (shards_of,), jnp.float32, least / len(pieces), top_value / len(pieces))
        return jnp.repeat(jnp.exp(draws), extent[axis_at] // shards_of).reshape((-1,) + (1,) * (len(extent) - axis_at - 1))

    gain = one(*pieces[0])
    for cut in pieces[1:]:
        gain = gain * one(*cut)
    return gain


def normal_values(rng, dims, scale, reach, pieces=(), kind=jnp.bfloat16):
    entries = jax.random.normal(rng, dims, jnp.float32) * scale
    if len(pieces) > 0:
        entries = block_levels(rng, dims, pieces, -0.22, 0.18) * entries
    return jnp.clip(entries, min=-reach, max=reach).astype(kind)


def setup_inputs(seed: int = 0) -> dict:
    streams_of = jax.random.split(jax.random.key(seed), 7)
    return {
        "token_values": normal_values(streams_of[0], (SEQUENCE_TOKENS, MIXER_HEADS * HEAD_DIM), 1.0, 6.0, ((0, 16), (1, 2))),
        "step_sizes": draw_step_sizes(jax.random.fold_in(streams_of[6], 71), 0),
        "log_rates": draw_log_rates(jax.random.fold_in(streams_of[6], 71), 0),
        "state_write": draw_state_write(jax.random.fold_in(streams_of[6], 71), 0),
        "state_read": normal_values(streams_of[4], (SEQUENCE_TOKENS, SHARED_GROUPS * STATE_SIZE), 1.0, 6.0, ((0, 32),)),
        "skip_gain": jnp.clip(0.5 + 1.0 * jax.random.uniform(streams_of[5], (MIXER_HEADS,), jnp.float32) ** block_levels(streams_of[5], (MIXER_HEADS,), ((0, 2),), -0.2, 0.2), 0.5, 1.5),
    }


def sequence_rows():
    half_rows = TOK_DEV // 2
    place = jnp.arange(SEQUENCE_TOKENS, dtype=jnp.int32)
    piece = place // half_rows
    offset = place % half_rows
    mirror = 2 * (SEQUENCE_TOKENS // TOK_DEV) - 1 - piece
    direct_row = piece * TOK_DEV + offset
    mirror_row = mirror * TOK_DEV + half_rows + offset
    return jnp.where(piece < SEQUENCE_TOKENS // TOK_DEV, direct_row, mirror_row).astype(jnp.int32)


def stored_positions():
    half_rows = TOK_DEV // 2
    row_index = jnp.arange(SEQUENCE_TOKENS, dtype=jnp.int32)
    owner = row_index // TOK_DEV
    inner = row_index % TOK_DEV
    lower_pos = owner * half_rows + inner
    upper_pos = (2 * (SEQUENCE_TOKENS // TOK_DEV) - 1 - owner) * half_rows + inner - half_rows
    return jnp.where(inner < half_rows, lower_pos, upper_pos).astype(jnp.int32)


def reference(token_values, step_sizes, log_rates, state_write, state_read, skip_gain):
    order = sequence_rows()
    per_group = MIXER_HEADS // SHARED_GROUPS
    blocks = SEQUENCE_TOKENS // SPAN
    values = jnp.take(token_values, order, axis=0).reshape(blocks, SPAN, MIXER_HEADS, HEAD_DIM)
    step_size = jnp.take(step_sizes, order, axis=1).astype(jnp.float32)
    log_decay = -step_size * jnp.exp(log_rates)[:, None]
    step_size = step_size.reshape(MIXER_HEADS, blocks, SPAN).transpose(1, 0, 2)
    log_decay = log_decay.reshape(MIXER_HEADS, blocks, SPAN).transpose(1, 0, 2)
    writes = jnp.take(state_write, order, axis=0).reshape(blocks, SPAN, SHARED_GROUPS, STATE_SIZE)
    reads = jnp.take(state_read, order, axis=0).reshape(blocks, SPAN, SHARED_GROUPS, STATE_SIZE)
    group_of = (jnp.arange(MIXER_HEADS, dtype=jnp.int32) // per_group).astype(jnp.int32)
    causal_mask = jnp.arange(SPAN)[:, None] >= jnp.arange(SPAN)[None, :]

    def one_block(state_carry, span_item):
        span_values, span_steps, span_decay, span_write, span_read = span_item
        cum = jnp.cumsum(span_decay, axis=-1)
        scores = jnp.einsum("ign,jgn->gij", span_read.astype(jnp.float32), span_write.astype(jnp.float32))
        head_scores = jnp.take(scores, group_of, axis=0)
        log_gap = cum[:, :, None] - cum[:, None, :]
        decay_table = jnp.where(causal_mask, jnp.exp(jnp.where(causal_mask, log_gap, 0.0)), 0.0)
        weights = (head_scores * decay_table * span_steps[:, None, :]).astype(jnp.bfloat16)
        weights = lax.optimization_barrier(weights).astype(jnp.float32)
        diagonal = jnp.einsum("hij,jhp->ihp", weights, span_values.astype(jnp.float32))
        head_read = jnp.take(span_read, group_of, axis=1).astype(jnp.float32)
        rounded = lax.optimization_barrier(state_carry.astype(jnp.bfloat16)).astype(jnp.float32)
        carried = jnp.einsum("ihn,hpn->ihp", head_read, rounded)
        growth = jnp.exp(cum).T[:, :, None]
        outputs = diagonal + growth * carried + skip_gain[None, :, None] * span_values.astype(jnp.float32)
        outputs = outputs.astype(jnp.bfloat16)
        tail_weight = jnp.exp(cum[:, -1:] - cum) * span_steps
        scaled = (span_values.astype(jnp.float32) * tail_weight.T[:, :, None]).astype(jnp.bfloat16)
        scaled = lax.optimization_barrier(scaled).astype(jnp.float32)
        head_write = jnp.take(span_write, group_of, axis=1).astype(jnp.float32)
        local_state = jnp.einsum("jhp,jhn->hpn", scaled, head_write)
        next_state = jnp.exp(cum[:, -1])[:, None, None] * state_carry + local_state
        return next_state, outputs

    start_state = jnp.zeros((MIXER_HEADS, HEAD_DIM, STATE_SIZE), jnp.float32)
    result = lax.scan(one_block, start_state, (values, step_size, log_decay, writes, reads))[1]
    in_sequence = result.reshape(SEQUENCE_TOKENS, MIXER_HEADS * HEAD_DIM)
    return jnp.take(in_sequence, stored_positions(), axis=0)
```

```python
import functools

import jax
import jax.numpy as jnp
from jax import lax
from jax.experimental import pallas as pl
from jax.experimental.pallas import tpu as pltpu
from jax.sharding import PartitionSpec as P

HEAD_DIM = 64
STATE_SIZE = 128
SPAN = 256
LOG2E = 1.4426950408889634
F32 = jnp.float32
BF16 = jnp.bfloat16


def split3(a):
    hi = a.astype(BF16)
    rest = a - hi.astype(F32)
    mid = rest.astype(BF16)
    low = (rest - mid.astype(F32)).astype(BF16)
    return hi, mid, low


def mixer_kernel(
    dims,
    x_hbm, step_hbm, rate_hbm, write_ref, read_ref, skip_hbm,
    out_ref,
    x_ref, step_ref, rate_ref, skip_ref,
    bmat, cmat, cum_row, step_row, cum_col, step_col, skip_row, scaled, local, diag,
    send1, recv1, dec1, decr1, chip, send2, recv2, dec2, decr2, slab,
    send3, recv3, send4, recv4, send5, recv5, enter,
    hs_b, hr_b, hs_c, hr_c, own_sem,
    s1, r1, s1d, r1d, s2, r2, s2d, r2d, s3, r3, s4, r4, s5, r5,
):
    n_ctx, n_head, heads, groups, chunk = dims
    per = heads // groups
    width = heads * HEAD_DIM
    half, quarter = width // 2, width // 4
    gw = per * HEAD_DIM
    n_chunk = quarter // chunk
    depth = n_ctx // 4
    units = 2 * groups
    part_rows = write_ref.shape[0]
    gcols = groups * STATE_SIZE

    ctx = lax.axis_index("ctx")
    hd = lax.axis_index("head")
    c = lax.rem(ctx, 2)
    y = lax.rem(ctx // 2, 2)
    z = ctx // 4
    core_peer = (ctx + 1 - 2 * c, hd)
    y_peer = (ctx + 2 - 4 * y, hd)
    up = (ctx + 4, hd)
    down = (ctx - 4, hd)

    def copy(src, dst, ssem, rsem, dev):
        return pltpu.make_async_remote_copy(
            src_ref=src, dst_ref=dst, send_sem=ssem, recv_sem=rsem,
            device_id=dev, device_id_type=pl.DeviceIdType.MESH,
        )

    loads = [
        pltpu.make_async_copy(src, dst, own_sem.at[2 + i])
        for i, (src, dst) in enumerate(
            ((rate_hbm, rate_ref), (skip_hbm, skip_ref), (step_hbm, step_ref), (x_hbm, x_ref))
        )
    ]
    for m in loads:
        m.start()

    barrier = pltpu.get_barrier_semaphore()

    def greet(dev):
        pl.semaphore_signal(barrier, inc=1, device_id=dev, device_id_type=pl.DeviceIdType.MESH)

    head_peers = [(ctx, lax.rem(hd + d, n_head)) for d in range(1, n_head)]
    for dev in head_peers + [core_peer, y_peer]:
        greet(dev)
    pl.when(z > 0)(lambda: greet(down))
    pl.when(z < depth - 1)(lambda: greet(up))
    expected = n_head - 1 + 2 + jnp.where(z > 0, 1, 0) + jnp.where(z < depth - 1, 1, 0)
    pl.semaphore_wait(barrier, expected)

    my_rows = pl.ds(pl.multiple_of(hd * part_rows, part_rows), part_rows)
    moves_b, moves_c = [], []
    for d in range(1, n_head):
        peer = lax.rem(hd + d, n_head)
        cols = pl.ds(pl.multiple_of(peer * gcols, gcols), gcols)
        moves_b.append(copy(write_ref.at[:, cols], bmat.at[my_rows, :], hs_b.at[d], hr_b.at[d], (ctx, peer)))
        moves_c.append(copy(read_ref.at[:, cols], cmat.at[my_rows, :], hs_c.at[d], hr_c.at[d], (ctx, peer)))
    for m in moves_b:
        m.start()
    for m in moves_c:
        m.start()
    my_cols = pl.ds(pl.multiple_of(hd * gcols, gcols), gcols)
    own_b = pltpu.make_async_copy(write_ref.at[:, my_cols], bmat.at[my_rows, :], own_sem.at[0])
    own_c = pltpu.make_async_copy(read_ref.at[:, my_cols], cmat.at[my_rows, :], own_sem.at[1])
    own_b.start()
    own_c.start()

    @pl.when(z == 0)
    def _():
        recv3[0] = jnp.zeros((STATE_SIZE, quarter), BF16)

    for m in loads[:3]:
        m.wait()

    ones = (
        lax.broadcasted_iota(jnp.int32, (SPAN, SPAN), 0)
        <= lax.broadcasted_iota(jnp.int32, (SPAN, SPAN), 1)
    ).astype(F32).astype(BF16)
    same = lax.broadcasted_iota(jnp.int32, (heads, heads), 0) == lax.broadcasted_iota(
        jnp.int32, (heads, heads), 1
    )
    rate = jnp.sum(jnp.where(same, jnp.exp(rate_ref[...]), 0.0), axis=1, keepdims=True)
    for g in range(groups):
        skip_row[g] = jnp.broadcast_to(skip_ref[0:1, g * per:(g + 1) * per], (8, per))
    for k in range(2):
        step = step_ref[:, k * SPAN:(k + 1) * SPAN].astype(F32)
        log_decay = -step * rate
        cum = sum(jnp.dot(piece, ones, preferred_element_type=F32) for piece in split3(log_decay)) * LOG2E
        for g in range(groups):
            u = k * groups + g
            cum_g = cum[g * per:(g + 1) * per, :]
            step_g = step[g * per:(g + 1) * per, :]
            cum_row[u] = cum_g
            step_row[u] = step_g
            cum_col[u] = cum_g.T
            step_col[u] = step_g.T

    left = lax.broadcasted_iota(jnp.int32, (SPAN, 128), 1) < HEAD_DIM

    def pair(cols, p):
        return jnp.where(left, cols[:, 2 * p:2 * p + 1], cols[:, 2 * p + 1:2 * p + 2])

    def scale_inputs(u, carry):
        k = u // groups
        g = lax.rem(u, groups)
        rows = pl.ds(pl.multiple_of(k * SPAN, SPAN), SPAN)
        base = pl.multiple_of(g * gw, gw)
        cums, steps = cum_col[u], step_col[u]
        for p in range(per // 2):
            ce, se = pair(cums, p), pair(steps, p)
            total = ce[SPAN - 1:SPAN, :]
            lanes = pl.ds(pl.multiple_of(base + p * 128, 128), 128)
            tail = jnp.exp2(total - ce) * se
            scaled[rows, lanes] = (x_ref[rows, lanes].astype(F32) * tail).astype(BF16)
            dec1[k, :, lanes] = jnp.broadcast_to(total, (8, 128))
        return carry

    def local_states(k):
        rows = slice(k * SPAN, (k + 1) * SPAN)

        def one_group(g, carry):
            lanes = pl.ds(pl.multiple_of(g * gw, gw), gw)
            bg = bmat[rows, pl.ds(pl.multiple_of(g * STATE_SIZE, STATE_SIZE), STATE_SIZE)]
            local[k, :, lanes] = lax.dot_general(
                bg, scaled[rows, lanes], (((0,), (0,)), ((), ())), preferred_element_type=F32
            )
            return carry

        lax.fori_loop(0, groups, one_group, 0)

    my_half = pl.multiple_of(c * half, half)
    peer_half = pl.multiple_of(half - c * half, half)
    my_q = pl.multiple_of(y * quarter, quarter)
    peer_q = pl.multiple_of(quarter - y * quarter, quarter)

    move1 = [copy(send1.at[k], recv1.at[k], s1.at[k], r1.at[k], core_peer) for k in range(2)]
    move1d = [copy(dec1.at[k], decr1.at[k], s1d.at[k], r1d.at[k], core_peer) for k in range(2)]
    move2 = [
        [
            copy(
                send2.at[k, :, pl.ds(i * chunk, chunk)], recv2.at[k, :, pl.ds(i * chunk, chunk)],
                s2.at[k, i], r2.at[k, i], y_peer,
            )
            for i in range(n_chunk)
        ]
        for k in range(2)
    ]
    move2d = [copy(dec2.at[k], decr2.at[k], s2d.at[k], r2d.at[k], y_peer) for k in range(2)]
    move4 = [
        [
            copy(
                send4.at[k, :, pl.ds(i * chunk, chunk)], recv4.at[k, :, pl.ds(i * chunk, chunk)],
                s4.at[k, i], r4.at[k, i], y_peer,
            )
            for i in range(n_chunk)
        ]
        for k in range(2)
    ]
    move5 = [
        [
            copy(
                send5.at[k, :, pl.ds(q, quarter)], recv5.at[k, :, pl.ds(q, quarter)],
                s5.at[k, i], r5.at[k, i], core_peer,
            )
            for i, q in enumerate((my_q, peer_q))
        ]
        for k in range(2)
    ]

    def send_local(k):
        send1[k] = local[k, :, pl.ds(peer_half, half)].astype(BF16)
        move1d[k].start()
        move1[k].start()

    later_c = (c == 1, c == 0)
    later_y = (y == 1, y == 0)

    def chip_totals(k):
        move1d[k].wait_recv()
        move1[k].wait_recv()
        own_log = dec1[k, :, pl.ds(my_half, half)]
        peer_log = decr1[k, :, pl.ds(my_half, half)]
        dec2[k] = own_log + peer_log
        own_by = jnp.where(later_c[k], 1.0, jnp.exp2(peer_log[0:1]))
        peer_by = jnp.where(later_c[k], jnp.exp2(own_log[0:1]), 1.0)
        chip[k] = own_by * local[k, :, pl.ds(my_half, half)] + peer_by * recv1[k].astype(F32)
        send2[k] = chip[k, :, pl.ds(peer_q, quarter)].astype(BF16)
        move2d[k].start()
        for m in move2[k]:
            m.start()

    def slab_chunk(k, i):
        move2[k][i].wait_recv()
        cols = slice(i * chunk, (i + 1) * chunk)
        lanes = pl.ds(pl.multiple_of(my_q + i * chunk, chunk), chunk)
        own_by = jnp.where(later_y[k], 1.0, jnp.exp2(decr2[k, 0:1, lanes]))
        peer_by = jnp.where(later_y[k], jnp.exp2(dec2[k, 0:1, lanes]), 1.0)
        slab[k, :, cols] = own_by * chip[k, :, lanes] + peer_by * recv2[k, :, cols].astype(F32)

    hops = [
        [
            copy(
                send3.at[k, :, pl.ds(i * chunk, chunk)], recv3.at[k, :, pl.ds(i * chunk, chunk)],
                s3.at[k, i], r3.at[k, i], (up, down)[k],
            )
            for i in range(n_chunk)
        ]
        for k in range(2)
    ]
    has_source = (z > 0, z < depth - 1)
    has_target = (z < depth - 1, z > 0)

    def run_chain(k):
        if k == 0:
            move2d[0].wait_recv()
        decay = jnp.exp2(dec2[k, 0:1, pl.ds(my_q, quarter)] + decr2[k, 0:1, pl.ds(my_q, quarter)])
        for i in range(n_chunk):
            cols = slice(i * chunk, (i + 1) * chunk)
            if k == 0:
                slab_chunk(0, i)
            pl.when(has_source[k])(hops[k][i].wait_recv)
            after = decay[:, cols] * recv3[k, :, cols].astype(F32) + slab[k, :, cols]
            send3[k, :, cols] = after.astype(BF16)
            if k == 0:

                @pl.when(z == depth - 1)
                def _():
                    recv3[1, :, cols] = after.astype(BF16)

            pl.when(has_target[k])(hops[k][i].start)
            if k == 1:
                send_chip_states(1, i)

    def send_chip_states(k, i):
        cols = slice(i * chunk, (i + 1) * chunk)
        lanes = pl.ds(pl.multiple_of(my_q + i * chunk, chunk), chunk)
        state = recv3[k, :, cols].astype(F32)
        first_log = jnp.where(later_y[k], decr2[k, 0:1, lanes], dec2[k, 0:1, lanes])
        first = jnp.where(later_y[k], recv2[k, :, cols].astype(F32), chip[k, :, lanes])
        second = jnp.exp2(first_log) * state + first
        send4[k, :, cols] = jnp.where(later_y[k], state, second).astype(BF16)
        move4[k][i].start()
        slab[k, :, cols] = jnp.where(later_y[k], second, state)

    def send_core_states(k, i):
        q = (my_q, peer_q)[i]
        if i == 1:
            for m in move4[k]:
                m.wait_recv()
        state = slab[k] if i == 0 else recv4[k].astype(F32)
        lanes = pl.ds(pl.multiple_of(my_half + q, quarter), quarter)
        here = pl.ds(q, quarter)
        first_log = jnp.where(later_c[k], decr1[k, 0:1, lanes], dec1[k, 0:1, lanes])
        first = jnp.where(later_c[k], recv1[k, :, here].astype(F32), local[k, :, lanes])
        second = jnp.exp2(first_log) * state + first
        send5[k, :, here] = jnp.where(later_c[k], state, second).astype(BF16)
        move5[k][i].start()
        enter[k, :, lanes] = jnp.where(later_c[k], second, state).astype(BF16)

    def gather_states(k):
        for m in move5[k]:
            m.wait_recv()
        enter[k, :, pl.ds(peer_half, half)] = recv5[k]

    quad = (
        lax.broadcasted_iota(jnp.int32, (128, 128), 0)
        >= lax.broadcasted_iota(jnp.int32, (128, 128), 1)
    )

    def diagonal(u, carry):
        k = u // groups
        g = lax.rem(u, groups)
        rows = pl.ds(pl.multiple_of(k * SPAN, SPAN), SPAN)
        gl = pl.ds(pl.multiple_of(g * STATE_SIZE, STATE_SIZE), STATE_SIZE)
        base = pl.multiple_of(g * gw, gw)
        scores = lax.dot_general(
            cmat[rows, gl], bmat[rows, gl], (((1,), (1,)), ((), ())), preferred_element_type=F32
        )
        s00 = jnp.where(quad, scores[:128, :128], 0.0)
        s10 = scores[128:, :128]
        s11 = jnp.where(quad, scores[128:, 128:], 0.0)
        cums, crow, srow = cum_col[u], cum_row[u], step_row[u]
        gains = skip_row[g, 0:1, :]
        for p in range(per // 2):
            lanes = pl.ds(pl.multiple_of(base + p * 128, 128), 128)
            xp = x_ref[rows, lanes]
            tops, lows = [], []
            for h in (2 * p, 2 * p + 1):
                c0, c1 = cums[:128, h:h + 1], cums[128:, h:h + 1]
                q0, q1 = crow[h:h + 1, :128], crow[h:h + 1, 128:]
                t0, t1 = srow[h:h + 1, :128], srow[h:h + 1, 128:]
                w00 = (s00 * jnp.exp2(jnp.minimum(c0 - q0, 0.0)) * t0).astype(BF16)
                w10 = (s10 * jnp.exp2(c1 - q0) * t0).astype(BF16)
                w11 = (s11 * jnp.exp2(jnp.minimum(c1 - q1, 0.0)) * t1).astype(BF16)
                tops.append(jnp.dot(w00, xp[:128], preferred_element_type=F32))
                lows.append(jnp.dot(jnp.concatenate([w10, w11], axis=1), xp, preferred_element_type=F32))
            gain = jnp.where(left[:1], gains[:, 2 * p:2 * p + 1], gains[:, 2 * p + 1:2 * p + 2])
            yt = jnp.where(left[:128], tops[0], tops[1]) + gain * xp[:128].astype(F32)
            yl = jnp.where(left[:128], lows[0], lows[1]) + gain * xp[128:].astype(F32)
            diag[rows, lanes] = jnp.concatenate([yt, yl], axis=0)
        return carry

    def finish(k):
        rows = slice(k * SPAN, (k + 1) * SPAN)

        def one_group(g, carry):
            u = k * groups + g
            base = pl.multiple_of(g * gw, gw)
            cg = cmat[rows, pl.ds(pl.multiple_of(g * STATE_SIZE, STATE_SIZE), STATE_SIZE)]
            cums = cum_col[u]
            for p in range(per // 2):
                lanes = pl.ds(pl.multiple_of(base + p * 128, 128), 128)
                carried = jnp.dot(cg, enter[k, :, lanes], preferred_element_type=F32)
                out_ref[rows, lanes] = (diag[rows, lanes] + jnp.exp2(pair(cums, p)) * carried).astype(BF16)
            return carry

        lax.fori_loop(0, groups, one_group, 0)

    loads[3].wait()
    lax.fori_loop(0, units, scale_inputs, 0)
    own_b.wait()
    for m in moves_b:
        m.wait_recv()
    local_states(0)
    send_local(0)
    local_states(1)
    send_local(1)
    own_c.wait()
    for m in moves_c:
        m.wait_recv()
    chip_totals(0)
    chip_totals(1)
    before = jnp.minimum(units, units // 4 + z + z // 2)
    middle = units - units // 8
    lax.fori_loop(0, before, diagonal, 0)
    run_chain(0)
    for i in range(n_chunk):
        send_chip_states(0, i)
    send_core_states(0, 0)
    move2d[1].wait_recv()
    for i in range(n_chunk):
        slab_chunk(1, i)
    lax.fori_loop(before, middle, diagonal, 0)
    run_chain(1)
    send_core_states(1, 0)
    send_core_states(0, 1)
    lax.fori_loop(middle, units, diagonal, 0)
    send_core_states(1, 1)
    gather_states(0)
    finish(0)
    gather_states(1)
    finish(1)

    for m in moves_b + moves_c + move1 + move1d + sum(move2 + move4 + move5, []) + move2d:
        m.wait_send()
    for k in range(2):
        for i in range(n_chunk):
            pl.when(has_target[k])(hops[k][i].wait_send)


def shards(n_ctx, n_head, token_values, step_sizes, log_rates, state_write, state_read, skip_gain):
    rows, width = token_values.shape
    heads = width // HEAD_DIM
    groups = state_write.shape[1] // STATE_SIZE // n_head
    per = heads // groups
    half, quarter = width // 2, width // 4
    chunk = min(256, quarter)
    n_chunk = quarter // chunk
    vm = pltpu.VMEM
    dma = pltpu.SemaphoreType.DMA
    n = STATE_SIZE
    scratch = [
        vm((rows, width), BF16), vm(step_sizes.shape, BF16), vm((1, heads), F32), vm((1, heads), F32),
        vm((rows, groups * n), BF16), vm((rows, groups * n), BF16),
        vm((2 * groups, per, SPAN), F32), vm((2 * groups, per, SPAN), F32),
        vm((2 * groups, SPAN, per), F32), vm((2 * groups, SPAN, per), F32),
        vm((groups, 8, per), F32),
        vm((rows, width), BF16), vm((2, n, width), F32), vm((rows, width), F32),
        vm((2, n, half), BF16), vm((2, n, half), BF16),
        vm((2, 8, width), F32), vm((2, 8, width), F32), vm((2, n, half), F32),
        vm((2, n, quarter), BF16), vm((2, n, quarter), BF16),
        vm((2, 8, half), F32), vm((2, 8, half), F32), vm((2, n, quarter), F32),
        vm((2, n, quarter), BF16), vm((2, n, quarter), BF16),
        vm((2, n, quarter), BF16), vm((2, n, quarter), BF16),
        vm((2, n, half), BF16), vm((2, n, half), BF16), vm((2, n, width), BF16),
        dma((n_head,)), dma((n_head,)), dma((n_head,)), dma((n_head,)), dma((6,)),
        dma((2,)), dma((2,)), dma((2,)), dma((2,)),
        dma((2, n_chunk)), dma((2, n_chunk)), dma((2,)), dma((2,)),
        dma((2, n_chunk)), dma((2, n_chunk)), dma((2, n_chunk)), dma((2, n_chunk)), dma((2, 2)), dma((2, 2)),
    ]
    return pl.pallas_call(
        functools.partial(mixer_kernel, (n_ctx, n_head, heads, groups, chunk)),
        out_shape=jax.ShapeDtypeStruct((rows, width), BF16),
        in_specs=[pl.BlockSpec(memory_space=pltpu.HBM)] * 6,
        out_specs=pl.BlockSpec(memory_space=pltpu.VMEM),
        scratch_shapes=scratch,
        compiler_params=pltpu.CompilerParams(
            collective_id=0, has_side_effects=True, vmem_limit_bytes=48 * 1024 * 1024
        ),
    )(
        token_values,
        step_sizes,
        log_rates[None],
        state_write,
        state_read,
        skip_gain[None],
    )


def solution(mesh):
    placed = (
        P("ctx", "head"),
        P("head", "ctx"),
        P("head"),
        P(("ctx", "head"), None),
        P(("ctx", "head"), None),
        P("head"),
    )
    body = functools.partial(shards, mesh.shape["ctx"], mesh.shape["head"])
    return jax.shard_map(body, mesh=mesh, in_specs=placed, out_specs=P("ctx", "head"), check_vma=False)
```

```python
import functools

import jax
import jax.numpy as jnp
from jax import lax
from jax.experimental import pallas as pl
from jax.experimental.pallas import tpu as pltpu
from jax.sharding import PartitionSpec as P

HEAD_DIM = 64
STATE_SIZE = 128
SPAN = 256
LOG2E = 1.4426950408889634
F32 = jnp.float32
BF16 = jnp.bfloat16


def split3(a):
    hi = a.astype(BF16)
    rest = a - hi.astype(F32)
    mid = rest.astype(BF16)
    low = (rest - mid.astype(F32)).astype(BF16)
    return hi, mid, low


def mixer_kernel(
    dims,
    x_hbm, step_hbm, rate_hbm, write_ref, read_ref, skip_hbm,
    out_ref,
    x_ref, step_ref, rate_ref, skip_ref,
    bmat, cmat, spread, cum_row, step_row, cum_col, tail2, grow2, skip_row, scaled, local, diag,
    dec1, decr1, dec2, decr2, la_send, la_recv, la,
    send1, recv1, chip, send2, recv2, slab, send3, recv3, send4, recv4, send5, enter,
    hs_b, hr_b, hs_c, hr_c, own_sem,
    s1, r1, s1d, r1d, s2, r2, s2d, r2d, s3, r3, sla, rla, s4, r4, s5, r5,
):
    n_ctx, n_head, heads, groups, chunk = dims
    per = heads // groups
    width = heads * HEAD_DIM
    half, quarter = width // 2, width // 4
    gw = per * HEAD_DIM
    block = 256
    n_chunk = quarter // chunk
    depth = n_ctx // 4
    units = 2 * groups
    part_rows = write_ref.shape[0]
    gcols = groups * STATE_SIZE

    ctx = lax.axis_index("ctx")
    hd = lax.axis_index("head")
    c = lax.rem(ctx, 2)
    y = lax.rem(ctx // 2, 2)
    z = ctx // 4
    core_peer = (ctx + 1 - 2 * c, hd)
    y_peer = (ctx + 2 - 4 * y, hd)
    up = (ctx + 4, hd)
    down = (ctx - 4, hd)

    def copy(src, dst, ssem, rsem, dev):
        return pltpu.make_async_remote_copy(
            src_ref=src, dst_ref=dst, send_sem=ssem, recv_sem=rsem,
            device_id=dev, device_id_type=pl.DeviceIdType.MESH,
        )

    def at(start, size, step=128):
        return pl.ds(pl.multiple_of(start, step), size)

    barrier = pltpu.get_barrier_semaphore()

    def greet(dev):
        pl.semaphore_signal(barrier, inc=1, device_id=dev, device_id_type=pl.DeviceIdType.MESH)

    head_peers = [(ctx, lax.rem(hd + d, n_head)) for d in range(1, n_head)]
    pl.when(z > 0)(lambda: greet(down))
    pl.when(z < depth - 1)(lambda: greet(up))
    for dev in [y_peer] + head_peers + [core_peer]:
        greet(dev)

    my_rows = at(hd * part_rows, part_rows, part_rows)
    my_cols = at(hd * gcols, gcols)
    loads = [
        pltpu.make_async_copy(src, dst, own_sem.at[2 + i])
        for i, (src, dst) in enumerate(
            ((rate_hbm, rate_ref), (skip_hbm, skip_ref), (step_hbm, step_ref), (x_hbm, x_ref))
        )
    ]
    own_b = pltpu.make_async_copy(write_ref.at[:, my_cols], bmat.at[my_rows, :], own_sem.at[0])
    own_c = pltpu.make_async_copy(read_ref.at[:, my_cols], cmat.at[my_rows, :], own_sem.at[1])
    for m in loads[:3] + [own_b, loads[3], own_c]:
        m.start()

    my_half, peer_half = c * half, half - c * half
    my_q, peer_q = y * quarter, quarter - y * quarter
    mine, others = 2 * c, 2 - 2 * c
    order = (others + 1 - y, mine + 1 - y, others + y, mine + y)

    @pl.when(z == 0)
    def _():
        recv3[0] = jnp.zeros((STATE_SIZE, quarter), BF16)

    @pl.when(z == depth - 1)
    def _():
        recv3[1] = jnp.zeros((STATE_SIZE, quarter), BF16)

    la[...] = jnp.zeros((3, 1, width), F32)

    spread[...] = (
        lax.rem(lax.broadcasted_iota(jnp.int32, (2 * per, gw), 0), per)
        == lax.broadcasted_iota(jnp.int32, (2 * per, gw), 1) // HEAD_DIM
    ).astype(F32).astype(BF16)
    ones = (
        lax.broadcasted_iota(jnp.int32, (SPAN, SPAN), 0)
        <= lax.broadcasted_iota(jnp.int32, (SPAN, SPAN), 1)
    ).astype(F32).astype(BF16)
    same = lax.broadcasted_iota(jnp.int32, (heads, heads), 0) == lax.broadcasted_iota(
        jnp.int32, (heads, heads), 1
    )

    def split2(a):
        hi = a.astype(BF16)
        return jnp.concatenate([hi, (a - hi.astype(F32)).astype(BF16)], axis=0)

    for m in loads[:3]:
        m.wait()
    rate = jnp.sum(jnp.where(same, jnp.exp(rate_ref[...]), 0.0), axis=1, keepdims=True)
    for g in range(groups):
        skip_row[g] = jnp.broadcast_to(skip_ref[0:1, g * per:(g + 1) * per], (8, per))
    for k in range(2):
        step = step_ref[:, k * SPAN:(k + 1) * SPAN].astype(F32)
        log_decay = -step * rate
        cum = sum(jnp.dot(piece, ones, preferred_element_type=F32) for piece in split3(log_decay)) * LOG2E
        tail = jnp.exp2(cum[:, SPAN - 1:SPAN] - cum) * step
        grow = jnp.exp2(cum)
        for g in range(groups):
            u = k * groups + g
            here = slice(g * per, (g + 1) * per)
            cum_row[u] = cum[here]
            step_row[u] = step[here]
            cols = cum[here].T
            cum_col[u] = cols
            tail2[u] = split2(tail[here])
            grow2[u] = split2(grow[here])
            ends = sum(
                jnp.dot(piece, spread[:per, :], preferred_element_type=F32) for piece in split3(cols[SPAN - 8:, :])
            )
            dec1[k, :, g * gw:(g + 1) * gw] = ends[7:8, :]

    expected = n_head - 1 + 2 + jnp.where(z > 0, 1, 0) + jnp.where(z < depth - 1, 1, 0)
    pl.semaphore_wait(barrier, expected)

    n_msg = 4 if groups == 4 else 1
    moves_b = [[] for _ in range(n_msg)]
    moves_c = []
    for d in range(1, n_head):
        peer = lax.rem(hd + d, n_head)
        for m in range(n_msg):
            if n_msg == 1:
                src, dst = at(peer * gcols, gcols), at(0, gcols)
            else:
                src, dst = (at((peer * groups * k + order[m]) * STATE_SIZE, STATE_SIZE) for k in (1, 0))
            moves_b[m].append(
                copy(write_ref.at[:, src], bmat.at[my_rows, dst], hs_b.at[d, m], hr_b.at[d, m], (ctx, peer))
            )
        cols = at(peer * gcols, gcols)
        moves_c.append(copy(read_ref.at[:, cols], cmat.at[my_rows, :], hs_c.at[d], hr_c.at[d], (ctx, peer)))
    move1d = copy(dec1, decr1, s1d, r1d, core_peer)
    move2d = copy(dec2, decr2, s2d, r2d, y_peer)
    move1d.start()
    for m in sum(moves_b, []) + moves_c:
        m.start()

    def move1(k, p):
        q = (peer_q, my_q)[p]
        return copy(send1.at[k, :, at(q, quarter)], recv1.at[k, :, at(q, quarter)], s1.at[k, p], r1.at[k, p], core_peer)

    def move2(k, i):
        cols = at(i * chunk, chunk)
        return copy(send2.at[k, :, cols], recv2.at[k, :, cols], s2.at[k, i], r2.at[k, i], y_peer)

    def hop(s, i):
        cols = at(i * chunk, chunk)
        dev = (ctx + 4 - 8 * s, hd)
        return copy(send3.at[s, :, cols], recv3.at[s, :, cols], s3.at[s, i], r3.at[s, i], dev)

    def move4(s, i):
        cols = at(i * chunk, chunk)
        return copy(send4.at[s, :, cols], recv4.at[s, :, cols], s4.at[s, i], r4.at[s, i], y_peer)

    def move5(s, p):
        q = (my_q, peer_q)[p]
        return copy(
            send5.at[s, :, at(q, quarter)], enter.at[s, :, at(my_half + q, quarter)],
            s5.at[s, p], r5.at[s, p], core_peer,
        )

    move_la = copy(la_send, la_recv, sla, rla, down)

    def scale_inputs(k, g):
        u = k * groups + g
        rows = at(k * SPAN, SPAN, SPAN)
        for j in range(gw // block):
            lanes = at(g * gw + j * block, block)
            by = lax.dot_general(
                tail2[u], spread[:, j * block:(j + 1) * block], (((0,), (0,)), ((), ())), preferred_element_type=F32
            )
            scaled[rows, lanes] = (x_ref[rows, lanes].astype(F32) * by).astype(BF16)

    def local_state(k, q):
        rows = at(k * SPAN, SPAN, SPAN)
        lanes = at(q * quarter, quarter)
        bg = bmat[rows, at((q * groups) // 4 * STATE_SIZE, STATE_SIZE)]
        local[k, :, lanes] = lax.dot_general(
            bg, scaled[rows, lanes], (((0,), (0,)), ((), ())), preferred_element_type=F32
        )

    def send_local(k, p):
        q = (peer_q, my_q)[p]
        send1[k, :, at(q, quarter)] = local[k, :, at(peer_half + q, quarter)].astype(BF16)
        move1(k, p).start()

    def chip_total(k, p):
        move1(k, p).wait_recv()
        later = c == 1 - k
        q = (peer_q, my_q)[p]
        for i in range(n_chunk):
            here, wide = at(q + i * chunk, chunk), at(my_half + q + i * chunk, chunk)
            own_by = jnp.where(later, 1.0, jnp.exp2(decr1[k, :, wide]))
            peer_by = jnp.where(later, jnp.exp2(dec1[k, :, wide]), 1.0)
            total = own_by * local[k, :, wide] + peer_by * recv1[k, :, here].astype(F32)
            cols = slice(i * chunk, (i + 1) * chunk)
            if p == 0:
                send2[k, :, cols] = total.astype(BF16)
                move2(k, i).start()
            else:
                chip[k, :, cols] = total

    def slab_chunk(k, i):
        move2(k, i).wait_recv()
        later = y == 1 - k
        cols, wide = at(i * chunk, chunk), at(my_half + my_q + i * chunk, chunk)
        own_by = jnp.where(later, 1.0, jnp.exp2(decr2[k, :, wide]))
        peer_by = jnp.where(later, jnp.exp2(dec2[k, :, wide]), 1.0)
        slab[k, :, cols] = own_by * chip[k, :, cols] + peer_by * recv2[k, :, cols].astype(F32)

    def chain_source(s):
        return jnp.where(s == 0, z > 0, z < depth - 1)

    def chain_target(s):
        return jnp.where(s == 0, z < depth - 1, z > 0)

    def both(second_part, by, first_part, extra):
        return jnp.where(second_part, by, 1.0) * first_part + jnp.where(second_part, 1.0, 0.0) * extra

    def core_expand(s, state, start):
        second_part = s == 1
        later = c == 1 - s
        here, wide = at(start, chunk), at(my_half + start, chunk)
        first_log = jnp.where(later, decr1[s, :, wide], dec1[s, :, wide])
        parts = [jnp.where(later, recv1[k, :, here].astype(F32), local[k, :, wide]) for k in range(2)]
        first = both(second_part, jnp.exp2(first_log + la[1, :, wide]), *parts)
        second = jnp.exp2(first_log) * state + first
        send5[s, :, here] = jnp.where(later, state, second).astype(BF16)
        enter[s, :, wide] = jnp.where(later, second, state).astype(BF16)

    def chain_step(s, i):
        second_part = s == 1
        cols, wide = at(i * chunk, chunk), at(my_half + my_q + i * chunk, chunk)
        pl.when(chain_source(s))(hop(s, i).wait_recv)
        state = recv3[s, :, cols].astype(F32)
        beyond = la[0, :, wide]

        @pl.when(chain_target(s))
        def _():
            log = dec2[s, :, wide] + decr2[s, :, wide]
            total = both(second_part, jnp.exp2(log + beyond), slab[0, :, cols], slab[1, :, cols])
            send3[s, :, cols] = (jnp.exp2(log) * state + total).astype(BF16)
            hop(s, i).start()

        later = y == 1 - s
        first_log = jnp.where(later, decr2[s, :, wide], dec2[s, :, wide])
        parts = [jnp.where(later, recv2[k, :, cols].astype(F32), chip[k, :, cols]) for k in range(2)]
        first = both(second_part, jnp.exp2(first_log + beyond), *parts)
        second = jnp.exp2(first_log) * state + first
        send4[s, :, cols] = jnp.where(later, state, second).astype(BF16)
        move4(s, i).start()
        core_expand(s, jnp.where(later, second, state), my_q + i * chunk)

    def expand_other(s):
        def one(i, carry):
            move4(s, i).wait_recv()
            core_expand(s, recv4[s, :, at(i * chunk, chunk)].astype(F32), peer_q + i * chunk)
            return carry

        lax.fori_loop(0, n_chunk, one, 0)
        move5(s, 1).start()

    def plane_logs():
        @pl.when(z < depth - 1)
        def _():
            move_la.wait_recv()
            la[0] = la_recv[...]

        beyond = la[0]
        plane = dec2[0] + decr2[0] + dec2[1] + decr2[1]

        @pl.when(z > 0)
        def _():
            la_send[...] = beyond + plane
            move_la.start()

        in_chip = beyond + jnp.where(y == 0, decr2[0] + decr2[1], 0.0)
        la[1] = in_chip
        la[2] = in_chip + jnp.where(c == 0, decr1[0] + decr1[1], 0.0)

    left = lax.broadcasted_iota(jnp.int32, (SPAN, 128), 1) < HEAD_DIM
    quad = (
        lax.broadcasted_iota(jnp.int32, (128, 128), 0)
        >= lax.broadcasted_iota(jnp.int32, (128, 128), 1)
    )
    own_k = hd // max(n_head // 2, 1)

    def diagonal(j, carry):
        k = lax.rem(own_k + j // groups, 2)
        g = lax.rem(j, groups)
        u = k * groups + g
        rows = at(k * SPAN, SPAN, SPAN)
        gl = at(g * STATE_SIZE, STATE_SIZE)
        base = g * gw
        scores = lax.dot_general(
            cmat[rows, gl], bmat[rows, gl], (((1,), (1,)), ((), ())), preferred_element_type=F32
        )
        s00 = jnp.where(quad, scores[:128, :128], 0.0)
        s10 = scores[128:, :128]
        s11 = jnp.where(quad, scores[128:, 128:], 0.0)
        cums, crow, srow = cum_col[u], cum_row[u], step_row[u]
        gains = skip_row[g, 0:1, :]
        for p in range(per // 2):
            lanes = at(base + p * 128, 128)
            xp = x_ref[rows, lanes]
            tops, lows = [], []
            for h in (2 * p, 2 * p + 1):
                c0, c1 = cums[:128, h:h + 1], cums[128:, h:h + 1]
                q0, q1 = crow[h:h + 1, :128], crow[h:h + 1, 128:]
                t0, t1 = srow[h:h + 1, :128], srow[h:h + 1, 128:]
                w00 = (s00 * jnp.exp2(jnp.minimum(c0 - q0, 0.0)) * t0).astype(BF16)
                w10 = (s10 * jnp.exp2(c1 - q0) * t0).astype(BF16)
                w11 = (s11 * jnp.exp2(jnp.minimum(c1 - q1, 0.0)) * t1).astype(BF16)
                tops.append(jnp.dot(w00, xp[:128], preferred_element_type=F32))
                lows.append(jnp.dot(jnp.concatenate([w10, w11], axis=1), xp, preferred_element_type=F32))
            gain = jnp.where(left[:1], gains[:, 2 * p:2 * p + 1], gains[:, 2 * p + 1:2 * p + 2])
            yt = jnp.where(left[:128], tops[0], tops[1]) + gain * xp[:128].astype(F32)
            yl = jnp.where(left[:128], lows[0], lows[1]) + gain * xp[128:].astype(F32)
            diag[rows, lanes] = jnp.concatenate([yt, yl], axis=0)
        return carry

    def diagonals(lower, upper):
        lax.fori_loop(lower, upper, diagonal, 0)

    def leaf(q):
        for j in range(quarter // block):
            lanes = at(q * quarter + j * block, block)
            log = la[2, :, lanes]
            after = jnp.exp2(log + dec1[0, :, lanes]) * enter[0, :, lanes].astype(F32)
            after += jnp.exp2(log) * local[0, :, lanes] + enter[1, :, lanes].astype(F32)
            enter[1, :, lanes] = after.astype(BF16)

    def finish(k, q):
        rows = slice(k * SPAN, (k + 1) * SPAN)
        g = (q * groups) // 4
        u = k * groups + g
        cg = cmat[rows, at(g * STATE_SIZE, STATE_SIZE)]
        for j in range(quarter // block):
            lanes = at(q * quarter + j * block, block)
            carried = jnp.dot(cg, enter[k, :, lanes], preferred_element_type=F32)
            by = lax.dot_general(
                grow2[u], spread[:, at(q * quarter + j * block - g * gw, block)], (((0,), (0,)), ((), ())),
                preferred_element_type=F32,
            )
            out_ref[rows, lanes] = (diag[rows, lanes] + by * carried).astype(BF16)

    def wait_b(messages):
        for m in messages:
            for move in moves_b[m]:
                move.wait_recv()

    def reduce_chip(k, waited):
        for p in range(2):
            if waited and n_msg == 4:
                wait_b((2 * p, 2 * p + 1))
            local_state(k, order[2 * p])
            send_local(k, p)
            local_state(k, order[2 * p + 1])
            if p == 1:
                chip_total(k, 0)
        chip_total(k, 1)

    own_first = n_head == 2
    own_b.wait()
    if not (own_first and n_msg == 4):
        wait_b(range(n_msg))
    loads[3].wait()
    other_k = 1 - own_k
    for g in range(groups):
        scale_inputs(own_k, g)
    move1d.wait_recv()
    dec2[...] = dec1[...] + decr1[...]
    move2d.start()
    reduce_chip(own_k, False)
    for g in range(groups):
        scale_inputs(other_k, g)
    own_c.wait()
    marks = [units // 4 + (i * units) // (2 * n_chunk) for i in range(n_chunk + 1)]
    if own_first:
        diagonals(0, marks[0])
    reduce_chip(other_k, own_first)
    move2d.wait_recv()
    pl.when(z == depth - 1)(plane_logs)
    lax.fori_loop(0, n_chunk, lambda i, carry: (slab_chunk(own_k, i), carry)[1], 0)
    pl.when(z == depth - 2)(plane_logs)
    at_end = jnp.logical_or(z == 0, z == depth - 1)
    first = (2 * z) // depth
    last = 1 - first
    if not own_first:
        for m in moves_c:
            m.wait_recv()
        diagonals(0, marks[0])
    for i in range(n_chunk):
        slab_chunk(other_k, i)

        @pl.when(at_end)
        def _():
            chain_step(first, i)

        if own_first and marks[i] <= groups < marks[i + 1]:
            for m in moves_c:
                m.wait_recv()
        diagonals(marks[i], marks[i + 1])
    pl.when(z < depth - 2)(plane_logs)

    @pl.when(jnp.logical_not(at_end))
    def _():
        lax.fori_loop(0, n_chunk, lambda i, carry: (chain_step(first, i), carry)[1], 0)

    move5(first, 0).start()
    half_way = jnp.where(at_end, units, marks[n_chunk])
    diagonals(marks[n_chunk], half_way)
    pl.when(at_end)(lambda: expand_other(first))

    @pl.when(z == 0)
    def _():
        for p in range(2):
            move5(0, p).wait_recv()
        lax.fori_loop(0, 4, lambda q, carry: (finish(0, q), carry)[1], 0)

    lax.fori_loop(0, n_chunk, lambda i, carry: (chain_step(last, i), carry)[1], 0)
    move5(last, 0).start()
    diagonals(half_way, units)
    pl.when(jnp.logical_not(at_end))(lambda: expand_other(first))

    @pl.when(z > 0)
    def _():
        for p in range(2):
            move5(first, p).wait_recv()

    for p, q in enumerate((order[3], order[2], order[1], order[0])):
        if p == 1:
            move5(last, 0).wait_recv()
        if p == 2:
            expand_other(last)
        if p == 3:
            move5(last, 1).wait_recv()
        leaf(q)
        pl.when(z > 0)(lambda: finish(0, q))
        finish(1, q)

    for m in sum(moves_b, []) + moves_c + [move1d, move2d]:
        m.wait_send()
    pl.when(z > 0)(move_la.wait_send)
    for k in range(2):
        for p in range(2):
            move1(k, p).wait_send()
            move5(k, p).wait_send()
        for i in range(n_chunk):
            move2(k, i).wait_send()
            move4(k, i).wait_send()
            pl.when(chain_target(k))(hop(k, i).wait_send)


def shards(n_ctx, n_head, token_values, step_sizes, log_rates, state_write, state_read, skip_gain):
    rows, width = token_values.shape
    heads = width // HEAD_DIM
    groups = state_write.shape[1] // STATE_SIZE // n_head
    per = heads // groups
    half, quarter = width // 2, width // 4
    chunk = min(256, quarter)
    n_chunk = quarter // chunk
    vm = pltpu.VMEM
    dma = pltpu.SemaphoreType.DMA
    n = STATE_SIZE
    scratch = [
        vm((rows, width), BF16), vm(step_sizes.shape, BF16), vm((1, heads), F32), vm((1, heads), F32),
        vm((rows, groups * n), BF16), vm((rows, groups * n), BF16), vm((2 * per, per * HEAD_DIM), BF16),
        vm((2 * groups, per, SPAN), F32), vm((2 * groups, per, SPAN), F32), vm((2 * groups, SPAN, per), F32),
        vm((2 * groups, 2 * per, SPAN), BF16), vm((2 * groups, 2 * per, SPAN), BF16), vm((groups, 8, per), F32),
        vm((rows, width), BF16), vm((2, n, width), F32), vm((rows, width), F32),
        vm((2, 1, width), F32), vm((2, 1, width), F32), vm((2, 1, width), F32), vm((2, 1, width), F32),
        vm((1, width), F32), vm((1, width), F32), vm((3, 1, width), F32),
        vm((2, n, half), BF16), vm((2, n, half), BF16), vm((2, n, quarter), F32),
        vm((2, n, quarter), BF16), vm((2, n, quarter), BF16), vm((2, n, quarter), F32),
        vm((2, n, quarter), BF16), vm((2, n, quarter), BF16), vm((2, n, quarter), BF16), vm((2, n, quarter), BF16),
        vm((2, n, half), BF16), vm((2, n, width), BF16),
        dma((n_head, 4)), dma((n_head, 4)), dma((n_head,)), dma((n_head,)), dma((6,)),
        dma((2, 2)), dma((2, 2)), dma(()), dma(()),
        dma((2, n_chunk)), dma((2, n_chunk)), dma(()), dma(()),
        dma((2, n_chunk)), dma((2, n_chunk)), dma(()), dma(()),
        dma((2, n_chunk)), dma((2, n_chunk)), dma((2, 2)), dma((2, 2)),
    ]
    return pl.pallas_call(
        functools.partial(mixer_kernel, (n_ctx, n_head, heads, groups, chunk)),
        out_shape=jax.ShapeDtypeStruct((rows, width), BF16),
        in_specs=[pl.BlockSpec(memory_space=pltpu.HBM)] * 6,
        out_specs=pl.BlockSpec(memory_space=pltpu.VMEM),
        scratch_shapes=scratch,
        compiler_params=pltpu.CompilerParams(
            collective_id=0, has_side_effects=True, vmem_limit_bytes=45 * 1024 * 1024
        ),
    )(
        *(
            pltpu.with_memory_space_constraint(a, pltpu.HBM)
            for a in (token_values, step_sizes, log_rates[None], state_write, state_read, skip_gain[None])
        )
    )


def solution(mesh):
    placed = (
        P("ctx", "head"),
        P("head", "ctx"),
        P("head"),
        P(("ctx", "head"), None),
        P(("ctx", "head"), None),
        P("head"),
    )
    body = functools.partial(shards, mesh.shape["ctx"], mesh.shape["head"])
    return jax.shard_map(body, mesh=mesh, in_specs=placed, out_specs=P("ctx", "head"), check_vma=False)
```

```python
import functools

import jax
import jax.numpy as jnp
from jax import lax
from jax.experimental import pallas as pl
from jax.experimental.pallas import tpu as pltpu
from jax.sharding import PartitionSpec as P

HEAD_DIM = 64
STATE_SIZE = 128
SPAN = 256
LOG2E = 1.4426950408889634
F32 = jnp.float32
BF16 = jnp.bfloat16


def split3(a):
    hi = a.astype(BF16)
    rest = a - hi.astype(F32)
    mid = rest.astype(BF16)
    low = (rest - mid.astype(F32)).astype(BF16)
    return hi, mid, low


def mixer_kernel(
    dims,
    x_hbm, step_hbm, rate_hbm, write_ref, read_ref, skip_hbm,
    out_ref,
    x_ref, step_ref, rate_ref, skip_ref,
    bmat, cmat, spread, cum_row, step_row, cum_col, tail2, grow2, skip_row, scaled, local, diag,
    dec1, decr1, dec2, decr2, la_send, la_recv, la,
    send1, recv1, chip, send2, recv2, slab, send3, recv3, send4, recv4, send5, enter,
    hs_b, hr_b, hs_c, hr_c, own_sem,
    s1, r1, s1d, r1d, s2, r2, s2d, r2d, s3, r3, sla, rla, s4, r4, s5, r5,
):
    n_ctx, n_head, heads, groups, chunk = dims
    per = heads // groups
    width = heads * HEAD_DIM
    half, quarter = width // 2, width // 4
    gw = per * HEAD_DIM
    block = 256
    n_chunk = quarter // chunk
    blocks = quarter // block
    depth = n_ctx // 4
    units = 2 * groups
    part_rows = write_ref.shape[0]
    gcols = groups * STATE_SIZE

    ctx = lax.axis_index("ctx")
    hd = lax.axis_index("head")
    c = lax.rem(ctx, 2)
    y = lax.rem(ctx // 2, 2)
    z = ctx // 4
    core_peer = (ctx + 1 - 2 * c, hd)
    y_peer = (ctx + 2 - 4 * y, hd)
    up = (ctx + 4, hd)
    down = (ctx - 4, hd)

    def copy(src, dst, ssem, rsem, dev):
        return pltpu.make_async_remote_copy(
            src_ref=src, dst_ref=dst, send_sem=ssem, recv_sem=rsem,
            device_id=dev, device_id_type=pl.DeviceIdType.MESH,
        )

    def at(start, size, step=128):
        return pl.ds(pl.multiple_of(start, step), size)

    barrier = pltpu.get_barrier_semaphore()

    def greet(dev):
        pl.semaphore_signal(barrier, inc=1, device_id=dev, device_id_type=pl.DeviceIdType.MESH)

    head_peers = [(ctx, lax.rem(hd + d, n_head)) for d in range(1, n_head)]
    pl.when(z > 0)(lambda: greet(down))
    pl.when(z < depth - 1)(lambda: greet(up))
    for dev in [y_peer] + head_peers + [core_peer]:
        greet(dev)

    my_rows = at(hd * part_rows, part_rows, part_rows)
    my_cols = at(hd * gcols, gcols)
    loads = [
        pltpu.make_async_copy(src, dst, own_sem.at[2 + i])
        for i, (src, dst) in enumerate(
            ((rate_hbm, rate_ref), (step_hbm, step_ref), (skip_hbm, skip_ref))
        )
    ]
    own_k = hd // max(n_head // 2, 1)
    other_k = 1 - own_k
    for i, k in enumerate((own_k, other_k)):
        rows = at(k * SPAN, SPAN, SPAN)
        loads.append(pltpu.make_async_copy(x_hbm.at[rows, :], x_ref.at[rows, :], own_sem.at[5 + i]))
    own_b = pltpu.make_async_copy(write_ref.at[:, my_cols], bmat.at[my_rows, :], own_sem.at[0])
    own_c = pltpu.make_async_copy(read_ref.at[:, my_cols], cmat.at[my_rows, :], own_sem.at[1])
    for m in loads[:3] + [own_b] + loads[3:] + [own_c]:
        m.start()

    my_half, peer_half = c * half, half - c * half
    my_q, peer_q = y * quarter, quarter - y * quarter
    mine, others = 2 * c, 2 - 2 * c
    order = (others + 1 - y, mine + 1 - y, others + y, mine + y)

    @pl.when(z == 0)
    def _():
        recv3[0] = jnp.zeros((STATE_SIZE, quarter), BF16)

    @pl.when(z == depth - 1)
    def _():
        recv3[1] = jnp.zeros((STATE_SIZE, quarter), BF16)

    la[...] = jnp.zeros((3, 1, width), F32)

    spread[...] = (
        lax.rem(lax.broadcasted_iota(jnp.int32, (2 * per, gw), 0), per)
        == lax.broadcasted_iota(jnp.int32, (2 * per, gw), 1) // HEAD_DIM
    ).astype(F32).astype(BF16)
    ones = (
        lax.broadcasted_iota(jnp.int32, (SPAN, SPAN), 0)
        <= lax.broadcasted_iota(jnp.int32, (SPAN, SPAN), 1)
    ).astype(F32).astype(BF16)
    same = lax.broadcasted_iota(jnp.int32, (heads, heads), 0) == lax.broadcasted_iota(
        jnp.int32, (heads, heads), 1
    )

    def split2(a):
        hi = a.astype(BF16)
        return jnp.concatenate([hi, (a - hi.astype(F32)).astype(BF16)], axis=0)

    for m in loads[:3]:
        m.wait()
    rate = jnp.sum(jnp.where(same, jnp.exp(rate_ref[...]), 0.0), axis=1, keepdims=True)
    for g in range(groups):
        skip_row[g] = jnp.broadcast_to(skip_ref[0:1, g * per:(g + 1) * per], (8, per))

    def block_logs(k):
        step = step_ref[:, at(k * SPAN, SPAN)].astype(F32)
        log_decay = -step * rate
        cum = sum(jnp.dot(piece, ones, preferred_element_type=F32) for piece in split3(log_decay)) * LOG2E
        tail = jnp.exp2(cum[:, SPAN - 1:SPAN] - cum) * step
        grow = jnp.exp2(cum)
        for g in range(groups):
            u = k * groups + g
            here = slice(g * per, (g + 1) * per)
            cum_row[u] = cum[here]
            step_row[u] = step[here]
            cols = cum[here].T
            cum_col[u] = cols
            tail2[u] = split2(tail[here])
            grow2[u] = split2(grow[here])
            ends = sum(
                jnp.dot(piece, spread[:per, :], preferred_element_type=F32) for piece in split3(cols[SPAN - 8:, :])
            )
            dec1[k, :, g * gw:(g + 1) * gw] = ends[7:8, :]

    block_logs(own_k)
    block_logs(other_k)
    expected = n_head - 1 + 2 + jnp.where(z > 0, 1, 0) + jnp.where(z < depth - 1, 1, 0)
    n_msg = 4 if groups == 4 else 1
    moves_b = [[] for _ in range(n_msg)]
    moves_c = []
    for d in range(1, n_head):
        peer = lax.rem(hd + d, n_head)
        for m in range(n_msg):
            if n_msg == 1:
                src, dst = at(peer * gcols, gcols), at(0, gcols)
            else:
                src, dst = (at((peer * groups * k + order[m]) * STATE_SIZE, STATE_SIZE) for k in (1, 0))
            moves_b[m].append(
                copy(write_ref.at[:, src], bmat.at[my_rows, dst], hs_b.at[d, m], hr_b.at[d, m], (ctx, peer))
            )
        cols = at(peer * gcols, gcols)
        moves_c.append(copy(read_ref.at[:, cols], cmat.at[my_rows, :], hs_c.at[d], hr_c.at[d], (ctx, peer)))
    move1d = copy(dec1, decr1, s1d, r1d, core_peer)
    move2d = copy(dec2, decr2, s2d, r2d, y_peer)

    def move1(k, p):
        q = (peer_q, my_q)[p]
        return copy(send1.at[k, :, at(q, quarter)], recv1.at[k, :, at(q, quarter)], s1.at[k, p], r1.at[k, p], core_peer)

    def move2(k, i):
        cols = at(i * chunk, chunk)
        return copy(send2.at[k, :, cols], recv2.at[k, :, cols], s2.at[k, i], r2.at[k, i], y_peer)

    def hop(s, i):
        cols = at(i * chunk, chunk)
        dev = (ctx + 4 - 8 * s, hd)
        return copy(send3.at[s, :, cols], recv3.at[s, :, cols], s3.at[s, i], r3.at[s, i], dev)

    def move4(s, i):
        cols = at(i * chunk, chunk)
        return copy(send4.at[s, :, cols], recv4.at[s, :, cols], s4.at[s, i], r4.at[s, i], y_peer)

    def move5(s, p):
        q, size = ((my_q, quarter), (peer_q, quarter // 2), (peer_q + quarter // 2, quarter // 2))[p]
        return copy(
            send5.at[s, :, at(q, size)], enter.at[s, :, at(my_half + q, size)],
            s5.at[s, p], r5.at[s, p], core_peer,
        )

    move_la = copy(la_send, la_recv, sla, rla, down)

    def scale_inputs(k, q):
        rows = at(k * SPAN, SPAN, SPAN)
        g = (q * groups) // 4
        for j in range(quarter // block):
            lanes = at(q * quarter + j * block, block)
            by = lax.dot_general(
                tail2[k * groups + g], spread[:, at(q * quarter + j * block - g * gw, block)],
                (((0,), (0,)), ((), ())), preferred_element_type=F32,
            )
            scaled[rows, lanes] = (x_ref[rows, lanes].astype(F32) * by).astype(BF16)

    def local_state(k, q):
        rows = at(k * SPAN, SPAN, SPAN)
        lanes = at(q * quarter, quarter)
        bg = bmat[rows, at((q * groups) // 4 * STATE_SIZE, STATE_SIZE)]
        local[k, :, lanes] = lax.dot_general(
            bg, scaled[rows, lanes], (((0,), (0,)), ((), ())), preferred_element_type=F32
        )

    def stage_local(k, p):
        q = (peer_q, my_q)[p]
        send1[k, :, at(q, quarter)] = local[k, :, at(peer_half + q, quarter)].astype(BF16)

    def chip_total(k, p):
        move1(k, p).wait_recv()
        later = c == 1 - k
        q = (peer_q, my_q)[p]
        for i in range(n_chunk):
            here, wide = at(q + i * chunk, chunk), at(my_half + q + i * chunk, chunk)
            own_by = jnp.where(later, 1.0, jnp.exp2(decr1[k, :, wide]))
            peer_by = jnp.where(later, jnp.exp2(dec1[k, :, wide]), 1.0)
            total = own_by * local[k, :, wide] + peer_by * recv1[k, :, here].astype(F32)
            cols = slice(i * chunk, (i + 1) * chunk)
            if p == 0:
                send2[k, :, cols] = total.astype(BF16)
                move2(k, i).start()
            else:
                chip[k, :, cols] = total

    def slab_chunk(k, i):
        move2(k, i).wait_recv()
        later = y == 1 - k
        cols, wide = at(i * chunk, chunk), at(my_half + my_q + i * chunk, chunk)
        own_by = jnp.where(later, 1.0, jnp.exp2(decr2[k, :, wide]))
        peer_by = jnp.where(later, jnp.exp2(dec2[k, :, wide]), 1.0)
        slab[k, :, cols] = own_by * chip[k, :, cols] + peer_by * recv2[k, :, cols].astype(F32)

    def chain_source(s):
        return jnp.where(s == 0, z > 0, z < depth - 1)

    def chain_target(s):
        return jnp.where(s == 0, z < depth - 1, z > 0)

    def both(second_part, by, first_part, extra):
        return jnp.where(second_part, by, 1.0) * first_part + jnp.where(second_part, 1.0, 0.0) * extra

    def core_expand(s, state, start):
        second_part = s == 1
        later = c == 1 - s
        here, wide = at(start, chunk), at(my_half + start, chunk)
        first_log = jnp.where(later, decr1[s, :, wide], dec1[s, :, wide])
        parts = [jnp.where(later, recv1[k, :, here].astype(F32), local[k, :, wide]) for k in range(2)]
        first = both(second_part, jnp.exp2(first_log + la[1, :, wide]), *parts)
        second = jnp.exp2(first_log) * state + first
        send5[s, :, here] = jnp.where(later, state, second).astype(BF16)
        enter[s, :, wide] = jnp.where(later, second, state).astype(BF16)

    def chain_step(s, i):
        second_part = s == 1
        cols, wide = at(i * chunk, chunk), at(my_half + my_q + i * chunk, chunk)
        pl.when(chain_source(s))(hop(s, i).wait_recv)
        state = recv3[s, :, cols].astype(F32)
        beyond = la[0, :, wide]

        @pl.when(chain_target(s))
        def _():
            log = dec2[s, :, wide] + decr2[s, :, wide]
            total = both(second_part, jnp.exp2(log + beyond), slab[0, :, cols], slab[1, :, cols])
            send3[s, :, cols] = (jnp.exp2(log) * state + total).astype(BF16)
            hop(s, i).start()

        later = y == 1 - s
        first_log = jnp.where(later, decr2[s, :, wide], dec2[s, :, wide])
        parts = [jnp.where(later, recv2[k, :, cols].astype(F32), chip[k, :, cols]) for k in range(2)]
        first = both(second_part, jnp.exp2(first_log + beyond), *parts)
        second = jnp.exp2(first_log) * state + first
        send4[s, :, cols] = jnp.where(later, state, second).astype(BF16)
        move4(s, i).start()
        core_expand(s, jnp.where(later, second, state), my_q + i * chunk)

    def expand_other(s):
        def one(i, carry):
            move4(s, i).wait_recv()
            core_expand(s, recv4[s, :, at(i * chunk, chunk)].astype(F32), peer_q + i * chunk)
            return carry

        for p in range(2):
            lax.fori_loop(p * n_chunk // 2, (p + 1) * n_chunk // 2, one, 0)
            move5(s, 1 + p).start()

    def plane_logs():
        @pl.when(z < depth - 1)
        def _():
            move_la.wait_recv()
            la[0] = la_recv[...]

        beyond = la[0]
        plane = dec2[0] + decr2[0] + dec2[1] + decr2[1]

        @pl.when(z > 0)
        def _():
            la_send[...] = beyond + plane
            move_la.start()

        in_chip = beyond + jnp.where(y == 0, decr2[0] + decr2[1], 0.0)
        la[1] = in_chip
        la[2] = in_chip + jnp.where(c == 0, decr1[0] + decr1[1], 0.0)

    left = lax.broadcasted_iota(jnp.int32, (SPAN, 128), 1) < HEAD_DIM
    quad = (
        lax.broadcasted_iota(jnp.int32, (128, 128), 0)
        >= lax.broadcasted_iota(jnp.int32, (128, 128), 1)
    )
    def diagonal(j, carry):
        k = lax.rem(own_k + j // groups, 2)
        g = lax.rem(j, groups)
        u = k * groups + g
        rows = at(k * SPAN, SPAN, SPAN)
        gl = at(g * STATE_SIZE, STATE_SIZE)
        base = g * gw
        scores = lax.dot_general(
            cmat[rows, gl], bmat[rows, gl], (((1,), (1,)), ((), ())), preferred_element_type=F32
        )
        s00 = jnp.where(quad, scores[:128, :128], 0.0)
        s10 = scores[128:, :128]
        s11 = jnp.where(quad, scores[128:, 128:], 0.0)
        cums, crow, srow = cum_col[u], cum_row[u], step_row[u]
        gains = skip_row[g, 0:1, :]
        for p in range(per // 2):
            lanes = at(base + p * 128, 128)
            xp = x_ref[rows, lanes]
            tops, lows = [], []
            for h in (2 * p, 2 * p + 1):
                c0, c1 = cums[:128, h:h + 1], cums[128:, h:h + 1]
                q0, q1 = crow[h:h + 1, :128], crow[h:h + 1, 128:]
                t0, t1 = srow[h:h + 1, :128], srow[h:h + 1, 128:]
                w00 = (s00 * jnp.exp2(jnp.minimum(c0 - q0, 0.0)) * t0).astype(BF16)
                w10 = (s10 * jnp.exp2(c1 - q0) * t0).astype(BF16)
                w11 = (s11 * jnp.exp2(jnp.minimum(c1 - q1, 0.0)) * t1).astype(BF16)
                tops.append(jnp.dot(w00, xp[:128], preferred_element_type=F32))
                lows.append(jnp.dot(jnp.concatenate([w10, w11], axis=1), xp, preferred_element_type=F32))
            gain = jnp.where(left[:1], gains[:, 2 * p:2 * p + 1], gains[:, 2 * p + 1:2 * p + 2])
            yt = jnp.where(left[:128], tops[0], tops[1]) + gain * xp[:128].astype(F32)
            yl = jnp.where(left[:128], lows[0], lows[1]) + gain * xp[128:].astype(F32)
            diag[rows, lanes] = jnp.concatenate([yt, yl], axis=0)
        return carry

    def diagonals(lower, upper):
        lax.fori_loop(lower, upper, diagonal, 0)

    def leaf(q, part):
        for j in part:
            lanes = at(q * quarter + j * block, block)
            log = la[2, :, lanes]
            after = jnp.exp2(log + dec1[0, :, lanes]) * enter[0, :, lanes].astype(F32)
            after += jnp.exp2(log) * local[0, :, lanes] + enter[1, :, lanes].astype(F32)
            enter[1, :, lanes] = after.astype(BF16)

    def finish(k, q, part):
        rows = slice(k * SPAN, (k + 1) * SPAN)
        g = (q * groups) // 4
        u = k * groups + g
        cg = cmat[rows, at(g * STATE_SIZE, STATE_SIZE)]
        for j in part:
            lanes = at(q * quarter + j * block, block)
            carried = jnp.dot(cg, enter[k, :, lanes], preferred_element_type=F32)
            by = lax.dot_general(
                grow2[u], spread[:, at(q * quarter + j * block - g * gw, block)], (((0,), (0,)), ((), ())),
                preferred_element_type=F32,
            )
            out_ref[rows, lanes] = (diag[rows, lanes] + by * carried).astype(BF16)

    def wait_b(messages):
        for m in messages:
            for move in moves_b[m]:
                move.wait_recv()

    def reduce_front(k, p):
        local_state(k, order[2 * p])
        stage_local(k, p)

    own_first = n_head == 2 and n_msg == 4
    own_b.wait()
    loads[3].wait()
    for q in order:
        scale_inputs(own_k, q)
    if own_first:
        reduce_front(own_k, 0)
    pl.semaphore_wait(barrier, expected)
    if not own_first:
        for m in sum(moves_b, []):
            m.start()
        wait_b(range(n_msg))
        reduce_front(own_k, 0)
    move1d.start()
    move1(own_k, 0).start()
    for m in (sum(moves_b, []) if own_first else []) + moves_c:
        m.start()
    local_state(own_k, order[1])
    reduce_front(own_k, 1)
    move1(own_k, 1).start()
    move1d.wait_recv()
    dec2[...] = dec1[...] + decr1[...]
    move2d.start()
    chip_total(own_k, 0)
    local_state(own_k, order[3])
    chip_total(own_k, 1)
    loads[4].wait()
    for q in order:
        scale_inputs(other_k, q)
    own_c.wait()
    before = units // 4 + units // 8
    marks = [before + (i + 1) // 2 * (units // 8) for i in range(n_chunk)] + [before + n_chunk // 2 * (units // 8)]
    if own_first:
        diagonals(0, units // 4)
    move2d.wait_recv()
    pl.when(z == depth - 1)(plane_logs)
    if own_first:
        wait_b((0, 1))
    reduce_front(other_k, 0)
    move1(other_k, 0).start()
    local_state(other_k, order[1])
    chip_total(other_k, 0)
    if own_first:
        wait_b((2, 3))
    reduce_front(other_k, 1)
    move1(other_k, 1).start()
    local_state(other_k, order[3])
    chip_total(other_k, 1)
    pl.when(z == depth - 2)(plane_logs)
    if own_first:
        diagonals(units // 4, before)
    lax.fori_loop(0, n_chunk, lambda i, carry: (slab_chunk(own_k, i), carry)[1], 0)
    pl.when(z == depth - 3)(plane_logs)
    at_end = jnp.logical_or(z == 0, z == depth - 1)
    first = (2 * z) // depth
    last = 1 - first
    if not own_first:
        for m in moves_c:
            m.wait_recv()
        diagonals(0, before)
    for i in range(n_chunk):
        slab_chunk(other_k, i)

        @pl.when(at_end)
        def _():
            chain_step(first, i)

        if own_first and marks[i] <= groups < marks[i + 1]:
            for m in moves_c:
                m.wait_recv()
        diagonals(marks[i], marks[i + 1])
    pl.when(z < depth - 3)(plane_logs)

    @pl.when(jnp.logical_not(at_end))
    def _():
        lax.fori_loop(0, n_chunk, lambda i, carry: (chain_step(first, i), carry)[1], 0)

    move5(first, 0).start()
    half_way = jnp.where(at_end, units, marks[n_chunk])
    diagonals(marks[n_chunk], half_way)
    pl.when(at_end)(lambda: expand_other(first))

    @pl.when(z == 0)
    def _():
        for p in range(3):
            move5(0, p).wait_recv()
        lax.fori_loop(0, 4, lambda q, carry: (finish(0, q, range(blocks)), carry)[1], 0)

    lax.fori_loop(0, n_chunk, lambda i, carry: (chain_step(last, i), carry)[1], 0)
    move5(last, 0).start()
    diagonals(half_way, units)
    pl.when(jnp.logical_not(at_end))(lambda: expand_other(first))

    @pl.when(z > 0)
    def _():
        for p in range(3):
            move5(first, p).wait_recv()

    def leave(q, part):
        leaf(q, part)
        pl.when(z > 0)(lambda: finish(0, q, part))
        finish(1, q, part)

    leave(order[3], range(blocks))
    move5(last, 0).wait_recv()
    leave(order[2], range(blocks))
    expand_other(last)
    leave(order[1], range(blocks))
    for p in range(2):
        move5(last, 1 + p).wait_recv()
        if blocks > 1:
            leave(order[0], range(p * blocks // 2, (p + 1) * blocks // 2))
        elif p == 1:
            leave(order[0], range(blocks))

    for m in sum(moves_b, []) + moves_c + [move1d, move2d]:
        m.wait_send()
    pl.when(z > 0)(move_la.wait_send)
    for k in range(2):
        for p in range(2):
            move1(k, p).wait_send()
        for p in range(3):
            move5(k, p).wait_send()
        for i in range(n_chunk):
            move2(k, i).wait_send()
            move4(k, i).wait_send()
            pl.when(chain_target(k))(hop(k, i).wait_send)


def shards(n_ctx, n_head, token_values, step_sizes, log_rates, state_write, state_read, skip_gain):
    rows, width = token_values.shape
    heads = width // HEAD_DIM
    groups = state_write.shape[1] // STATE_SIZE // n_head
    per = heads // groups
    half, quarter = width // 2, width // 4
    chunk = min(256, quarter)
    n_chunk = quarter // chunk
    vm = pltpu.VMEM
    dma = pltpu.SemaphoreType.DMA
    n = STATE_SIZE
    scratch = [
        vm((rows, width), BF16), vm(step_sizes.shape, BF16), vm((1, heads), F32), vm((1, heads), F32),
        vm((rows, groups * n), BF16), vm((rows, groups * n), BF16), vm((2 * per, per * HEAD_DIM), BF16),
        vm((2 * groups, per, SPAN), F32), vm((2 * groups, per, SPAN), F32), vm((2 * groups, SPAN, per), F32),
        vm((2 * groups, 2 * per, SPAN), BF16), vm((2 * groups, 2 * per, SPAN), BF16), vm((groups, 8, per), F32),
        vm((rows, width), BF16), vm((2, n, width), F32), vm((rows, width), F32),
        vm((2, 1, width), F32), vm((2, 1, width), F32), vm((2, 1, width), F32), vm((2, 1, width), F32),
        vm((1, width), F32), vm((1, width), F32), vm((3, 1, width), F32),
        vm((2, n, half), BF16), vm((2, n, half), BF16), vm((2, n, quarter), F32),
        vm((2, n, quarter), BF16), vm((2, n, quarter), BF16), vm((2, n, quarter), F32),
        vm((2, n, quarter), BF16), vm((2, n, quarter), BF16), vm((2, n, quarter), BF16), vm((2, n, quarter), BF16),
        vm((2, n, half), BF16), vm((2, n, width), BF16),
        dma((n_head, 4)), dma((n_head, 4)), dma((n_head,)), dma((n_head,)), dma((7,)),
        dma((2, 2)), dma((2, 2)), dma(()), dma(()),
        dma((2, n_chunk)), dma((2, n_chunk)), dma(()), dma(()),
        dma((2, n_chunk)), dma((2, n_chunk)), dma(()), dma(()),
        dma((2, n_chunk)), dma((2, n_chunk)), dma((2, 3)), dma((2, 3)),
    ]
    return pl.pallas_call(
        functools.partial(mixer_kernel, (n_ctx, n_head, heads, groups, chunk)),
        out_shape=jax.ShapeDtypeStruct((rows, width), BF16),
        in_specs=[pl.BlockSpec(memory_space=pltpu.HBM)] * 6,
        out_specs=pl.BlockSpec(memory_space=pltpu.VMEM),
        scratch_shapes=scratch,
        compiler_params=pltpu.CompilerParams(
            collective_id=0, has_side_effects=True, vmem_limit_bytes=45 * 1024 * 1024
        ),
    )(
        *(
            pltpu.with_memory_space_constraint(a, pltpu.HBM)
            for a in (token_values, step_sizes, log_rates[None], state_write, state_read, skip_gain[None])
        )
    )


def solution(mesh):
    placed = (
        P("ctx", "head"),
        P("head", "ctx"),
        P("head"),
        P(("ctx", "head"), None),
        P(("ctx", "head"), None),
        P("head"),
    )
    body = functools.partial(shards, mesh.shape["ctx"], mesh.shape["head"])
    return jax.shard_map(body, mesh=mesh, in_specs=placed, out_specs=P("ctx", "head"), check_vma=False)
```

```python
import functools

import jax
import jax.numpy as jnp
from jax import lax
from jax.experimental import pallas as pl
from jax.experimental.pallas import tpu as pltpu
from jax.sharding import PartitionSpec as P

HEAD_DIM = 64
STATE_SIZE = 128
SPAN = 256
LOG2E = 1.4426950408889634
F32 = jnp.float32
BF16 = jnp.bfloat16


def split3(a):
    hi = a.astype(BF16)
    rest = a - hi.astype(F32)
    mid = rest.astype(BF16)
    low = (rest - mid.astype(F32)).astype(BF16)
    return hi, mid, low


def mixer_kernel(
    dims,
    x_hbm, step_hbm, rate_hbm, write_ref, read_ref, skip_hbm,
    out_ref,
    x_ref, step_ref, rate_ref, skip_ref,
    bmat, cmat, spread, cum_row, step_row, cum_col, tail2, grow2, skip_row, scaled, local, diag,
    dec1, decr1, dec2, decr2, la_send, la_recv, la,
    send1, recv1, chip, send2, recv2, slab, send3, recv3, send4, recv4, send5, enter,
    hs_b, hr_b, hs_c, hr_c, own_sem,
    s1, r1, s1d, r1d, s2, r2, s2d, r2d, s3, r3, sla, rla, s4, r4, s5, r5,
):
    n_ctx, n_head, heads, groups, chunk = dims
    per = heads // groups
    width = heads * HEAD_DIM
    half, quarter = width // 2, width // 4
    gw = per * HEAD_DIM
    block = 256
    n_chunk = quarter // chunk
    blocks = quarter // block
    depth = n_ctx // 4
    units = 2 * groups
    part_rows = write_ref.shape[0]
    gcols = groups * STATE_SIZE

    ctx = lax.axis_index("ctx")
    hd = lax.axis_index("head")
    c = lax.rem(ctx, 2)
    y = lax.rem(ctx // 2, 2)
    z = ctx // 4
    core_peer = (ctx + 1 - 2 * c, hd)
    y_peer = (ctx + 2 - 4 * y, hd)
    up = (ctx + 4, hd)
    down = (ctx - 4, hd)

    def copy(src, dst, ssem, rsem, dev):
        return pltpu.make_async_remote_copy(
            src_ref=src, dst_ref=dst, send_sem=ssem, recv_sem=rsem,
            device_id=dev, device_id_type=pl.DeviceIdType.MESH,
        )

    def at(start, size, step=128):
        return pl.ds(pl.multiple_of(start, step), size)

    barrier = pltpu.get_barrier_semaphore()

    def greet(dev):
        pl.semaphore_signal(barrier, inc=1, device_id=dev, device_id_type=pl.DeviceIdType.MESH)

    head_peers = [(ctx, lax.rem(hd + d, n_head)) for d in range(1, n_head)]
    pl.when(z > 0)(lambda: greet(down))
    pl.when(z < depth - 1)(lambda: greet(up))
    for dev in [y_peer] + head_peers + [core_peer]:
        greet(dev)

    my_rows = at(hd * part_rows, part_rows, part_rows)
    my_cols = at(hd * gcols, gcols)
    loads = [
        pltpu.make_async_copy(src, dst, own_sem.at[2 + i])
        for i, (src, dst) in enumerate(
            ((rate_hbm, rate_ref), (step_hbm, step_ref), (skip_hbm, skip_ref))
        )
    ]
    own_k = hd // max(n_head // 2, 1)
    other_k = 1 - own_k
    for i, k in enumerate((own_k, other_k)):
        rows = at(k * SPAN, SPAN, SPAN)
        loads.append(pltpu.make_async_copy(x_hbm.at[rows, :], x_ref.at[rows, :], own_sem.at[5 + i]))
    own_b = pltpu.make_async_copy(write_ref.at[:, my_cols], bmat.at[my_rows, :], own_sem.at[0])
    own_c = pltpu.make_async_copy(read_ref.at[:, my_cols], cmat.at[my_rows, :], own_sem.at[1])
    for m in loads[:3] + [own_b] + loads[3:] + [own_c]:
        m.start()

    my_half, peer_half = c * half, half - c * half
    my_q, peer_q = y * quarter, quarter - y * quarter
    mine, others = 2 * c, 2 - 2 * c
    order = (others + 1 - y, mine + 1 - y, others + y, mine + y)

    @pl.when(z == 0)
    def _():
        recv3[0] = jnp.zeros((STATE_SIZE, quarter), BF16)

    @pl.when(z == depth - 1)
    def _():
        recv3[1] = jnp.zeros((STATE_SIZE, quarter), BF16)

    la[...] = jnp.zeros((3, 1, width), F32)

    spread[...] = (
        lax.rem(lax.broadcasted_iota(jnp.int32, (2 * per, gw), 0), per)
        == lax.broadcasted_iota(jnp.int32, (2 * per, gw), 1) // HEAD_DIM
    ).astype(F32).astype(BF16)
    ones = (
        lax.broadcasted_iota(jnp.int32, (SPAN, SPAN), 0)
        <= lax.broadcasted_iota(jnp.int32, (SPAN, SPAN), 1)
    ).astype(F32).astype(BF16)
    same = lax.broadcasted_iota(jnp.int32, (heads, heads), 0) == lax.broadcasted_iota(
        jnp.int32, (heads, heads), 1
    )

    def split2(a):
        hi = a.astype(BF16)
        return jnp.concatenate([hi, (a - hi.astype(F32)).astype(BF16)], axis=0)

    for m in loads[:3]:
        m.wait()
    rate = jnp.sum(jnp.where(same, jnp.exp(rate_ref[...]), 0.0), axis=1, keepdims=True)
    for g in range(groups):
        skip_row[g] = jnp.broadcast_to(skip_ref[0:1, g * per:(g + 1) * per], (8, per))

    def block_logs(k):
        step = step_ref[:, at(k * SPAN, SPAN)].astype(F32)
        log_decay = -step * rate
        cum = sum(jnp.dot(piece, ones, preferred_element_type=F32) for piece in split3(log_decay)) * LOG2E
        tail = jnp.exp2(cum[:, SPAN - 1:SPAN] - cum) * step
        grow = jnp.exp2(cum)
        for g in range(groups):
            u = k * groups + g
            here = slice(g * per, (g + 1) * per)
            cum_row[u] = cum[here]
            step_row[u] = step[here]
            cols = cum[here].T
            cum_col[u] = cols
            tail2[u] = split2(tail[here])
            grow2[u] = split2(grow[here])
            ends = sum(
                jnp.dot(piece, spread[:per, :], preferred_element_type=F32) for piece in split3(cols[SPAN - 8:, :])
            )
            dec1[k, :, g * gw:(g + 1) * gw] = ends[7:8, :]

    block_logs(own_k)
    block_logs(other_k)
    expected = n_head - 1 + 2 + jnp.where(z > 0, 1, 0) + jnp.where(z < depth - 1, 1, 0)
    n_msg = 4 if groups == 4 else 1
    moves_b = [[] for _ in range(n_msg)]
    moves_c = []
    for d in range(1, n_head):
        peer = lax.rem(hd + d, n_head)
        for m in range(n_msg):
            if n_msg == 1:
                src, dst = at(peer * gcols, gcols), at(0, gcols)
            else:
                src, dst = (at((peer * groups * k + order[m]) * STATE_SIZE, STATE_SIZE) for k in (1, 0))
            moves_b[m].append(
                copy(write_ref.at[:, src], bmat.at[my_rows, dst], hs_b.at[d, m], hr_b.at[d, m], (ctx, peer))
            )
        cols = at(peer * gcols, gcols)
        moves_c.append(copy(read_ref.at[:, cols], cmat.at[my_rows, :], hs_c.at[d], hr_c.at[d], (ctx, peer)))
    move1d = copy(dec1, decr1, s1d, r1d, core_peer)
    move2d = copy(dec2, decr2, s2d, r2d, y_peer)

    def move1(k, p):
        q = (peer_q, my_q)[p]
        return copy(send1.at[k, :, at(q, quarter)], recv1.at[k, :, at(q, quarter)], s1.at[k, p], r1.at[k, p], core_peer)

    def move2(k, i):
        cols = at(i * chunk, chunk)
        return copy(send2.at[k, :, cols], recv2.at[k, :, cols], s2.at[k, i], r2.at[k, i], y_peer)

    def hop(s, i):
        cols = at(i * chunk, chunk)
        dev = (ctx + 4 - 8 * s, hd)
        return copy(send3.at[s, :, cols], recv3.at[s, :, cols], s3.at[s, i], r3.at[s, i], dev)

    def move4(s, i):
        cols = at(i * chunk, chunk)
        return copy(send4.at[s, :, cols], recv4.at[s, :, cols], s4.at[s, i], r4.at[s, i], y_peer)

    def move5(s, p):
        q, size = (my_q, quarter) if isinstance(p, str) else (peer_q + p * chunk, chunk)
        p = n_chunk if isinstance(p, str) else p
        return copy(
            send5.at[s, :, at(q, size)], enter.at[s, :, at(my_half + q, size)],
            s5.at[s, p], r5.at[s, p], core_peer,
        )

    move_la = copy(la_send, la_recv, sla, rla, down)

    def scale_inputs(k, q):
        rows = at(k * SPAN, SPAN, SPAN)
        g = (q * groups) // 4
        for j in range(quarter // block):
            lanes = at(q * quarter + j * block, block)
            by = lax.dot_general(
                tail2[k * groups + g], spread[:, at(q * quarter + j * block - g * gw, block)],
                (((0,), (0,)), ((), ())), preferred_element_type=F32,
            )
            scaled[rows, lanes] = (x_ref[rows, lanes].astype(F32) * by).astype(BF16)

    def local_state(k, q):
        rows = at(k * SPAN, SPAN, SPAN)
        lanes = at(q * quarter, quarter)
        bg = bmat[rows, at((q * groups) // 4 * STATE_SIZE, STATE_SIZE)]
        local[k, :, lanes] = lax.dot_general(
            bg, scaled[rows, lanes], (((0,), (0,)), ((), ())), preferred_element_type=F32
        )

    def stage_local(k, p):
        q = (peer_q, my_q)[p]
        send1[k, :, at(q, quarter)] = local[k, :, at(peer_half + q, quarter)].astype(BF16)

    def chip_total(k, p):
        move1(k, p).wait_recv()
        later = c == 1 - k
        q = (peer_q, my_q)[p]
        for i in range(n_chunk):
            here, wide = at(q + i * chunk, chunk), at(my_half + q + i * chunk, chunk)
            own_by = jnp.where(later, 1.0, jnp.exp2(decr1[k, :, wide]))
            peer_by = jnp.where(later, jnp.exp2(dec1[k, :, wide]), 1.0)
            total = own_by * local[k, :, wide] + peer_by * recv1[k, :, here].astype(F32)
            cols = slice(i * chunk, (i + 1) * chunk)
            if p == 0:
                send2[k, :, cols] = total.astype(BF16)
                move2(k, i).start()
            else:
                chip[k, :, cols] = total

    def slab_chunk(k, i):
        move2(k, i).wait_recv()
        later = y == 1 - k
        cols, wide = at(i * chunk, chunk), at(my_half + my_q + i * chunk, chunk)
        own_by = jnp.where(later, 1.0, jnp.exp2(decr2[k, :, wide]))
        peer_by = jnp.where(later, jnp.exp2(dec2[k, :, wide]), 1.0)
        slab[k, :, cols] = own_by * chip[k, :, cols] + peer_by * recv2[k, :, cols].astype(F32)

    def chain_source(s):
        return jnp.where(s == 0, z > 0, z < depth - 1)

    def chain_target(s):
        return jnp.where(s == 0, z < depth - 1, z > 0)

    def both(second_part, by, first_part, extra):
        return jnp.where(second_part, by, 1.0) * first_part + jnp.where(second_part, 1.0, 0.0) * extra

    def core_expand(s, state, start):
        second_part = s == 1
        later = c == 1 - s
        here, wide = at(start, chunk), at(my_half + start, chunk)
        first_log = jnp.where(later, decr1[s, :, wide], dec1[s, :, wide])
        parts = [jnp.where(later, recv1[k, :, here].astype(F32), local[k, :, wide]) for k in range(2)]
        first = both(second_part, jnp.exp2(first_log + la[1, :, wide]), *parts)
        second = jnp.exp2(first_log) * state + first
        send5[s, :, here] = jnp.where(later, state, second).astype(BF16)
        enter[s, :, wide] = jnp.where(later, second, state).astype(BF16)

    def chain_step(s, i):
        second_part = s == 1
        cols, wide = at(i * chunk, chunk), at(my_half + my_q + i * chunk, chunk)
        pl.when(chain_source(s))(hop(s, i).wait_recv)
        state = recv3[s, :, cols].astype(F32)
        beyond = la[0, :, wide]

        @pl.when(chain_target(s))
        def _():
            log = dec2[s, :, wide] + decr2[s, :, wide]
            total = both(second_part, jnp.exp2(log + beyond), slab[0, :, cols], slab[1, :, cols])
            send3[s, :, cols] = (jnp.exp2(log) * state + total).astype(BF16)
            hop(s, i).start()

        later = y == 1 - s
        first_log = jnp.where(later, decr2[s, :, wide], dec2[s, :, wide])
        parts = [jnp.where(later, recv2[k, :, cols].astype(F32), chip[k, :, cols]) for k in range(2)]
        first = both(second_part, jnp.exp2(first_log + beyond), *parts)
        second = jnp.exp2(first_log) * state + first
        send4[s, :, cols] = jnp.where(later, state, second).astype(BF16)
        move4(s, i).start()
        core_expand(s, jnp.where(later, second, state), my_q + i * chunk)

    def expand_chunk(s, i):
        move4(s, i).wait_recv()
        core_expand(s, recv4[s, :, at(i * chunk, chunk)].astype(F32), peer_q + i * chunk)
        move5(s, i).start()

    def expand_other(s):
        lax.fori_loop(0, n_chunk, lambda i, carry: (expand_chunk(s, i), carry)[1], 0)

    def plane_logs():
        @pl.when(z < depth - 1)
        def _():
            move_la.wait_recv()
            la[0] = la_recv[...]

        beyond = la[0]
        plane = dec2[0] + decr2[0] + dec2[1] + decr2[1]

        @pl.when(z > 0)
        def _():
            la_send[...] = beyond + plane
            move_la.start()

        in_chip = beyond + jnp.where(y == 0, decr2[0] + decr2[1], 0.0)
        la[1] = in_chip
        la[2] = in_chip + jnp.where(c == 0, decr1[0] + decr1[1], 0.0)

    left = lax.broadcasted_iota(jnp.int32, (SPAN, 128), 1) < HEAD_DIM
    quad = (
        lax.broadcasted_iota(jnp.int32, (128, 128), 0)
        >= lax.broadcasted_iota(jnp.int32, (128, 128), 1)
    )
    def diagonal(j, carry):
        k = lax.rem(own_k + j // groups, 2)
        g = lax.rem(j, groups)
        u = k * groups + g
        rows = at(k * SPAN, SPAN, SPAN)
        gl = at(g * STATE_SIZE, STATE_SIZE)
        base = g * gw
        scores = lax.dot_general(
            cmat[rows, gl], bmat[rows, gl], (((1,), (1,)), ((), ())), preferred_element_type=F32
        )
        s00 = jnp.where(quad, scores[:128, :128], 0.0)
        s10 = scores[128:, :128]
        s11 = jnp.where(quad, scores[128:, 128:], 0.0)
        cums, crow, srow = cum_col[u], cum_row[u], step_row[u]
        gains = skip_row[g, 0:1, :]
        for p in range(per // 2):
            lanes = at(base + p * 128, 128)
            xp = x_ref[rows, lanes]
            tops, lows = [], []
            for h in (2 * p, 2 * p + 1):
                c0, c1 = cums[:128, h:h + 1], cums[128:, h:h + 1]
                q0, q1 = crow[h:h + 1, :128], crow[h:h + 1, 128:]
                t0, t1 = srow[h:h + 1, :128], srow[h:h + 1, 128:]
                w00 = (s00 * jnp.exp2(jnp.minimum(c0 - q0, 0.0)) * t0).astype(BF16)
                w10 = (s10 * jnp.exp2(c1 - q0) * t0).astype(BF16)
                w11 = (s11 * jnp.exp2(jnp.minimum(c1 - q1, 0.0)) * t1).astype(BF16)
                tops.append(jnp.dot(w00, xp[:128], preferred_element_type=F32))
                lows.append(jnp.dot(jnp.concatenate([w10, w11], axis=1), xp, preferred_element_type=F32))
            gain = jnp.where(left[:1], gains[:, 2 * p:2 * p + 1], gains[:, 2 * p + 1:2 * p + 2])
            yt = jnp.where(left[:128], tops[0], tops[1]) + gain * xp[:128].astype(F32)
            yl = jnp.where(left[:128], lows[0], lows[1]) + gain * xp[128:].astype(F32)
            diag[rows, lanes] = jnp.concatenate([yt, yl], axis=0)
        return carry

    def diagonals(lower, upper):
        lax.fori_loop(lower, upper, diagonal, 0)

    def leaf(q, part):
        for j in part:
            lanes = at(q * quarter + j * block, block)
            log = la[2, :, lanes]
            after = jnp.exp2(log + dec1[0, :, lanes]) * enter[0, :, lanes].astype(F32)
            after += jnp.exp2(log) * local[0, :, lanes] + enter[1, :, lanes].astype(F32)
            enter[1, :, lanes] = after.astype(BF16)

    def finish(k, q, part):
        rows = slice(k * SPAN, (k + 1) * SPAN)
        g = (q * groups) // 4
        u = k * groups + g
        cg = cmat[rows, at(g * STATE_SIZE, STATE_SIZE)]
        for j in part:
            lanes = at(q * quarter + j * block, block)
            carried = jnp.dot(cg, enter[k, :, lanes], preferred_element_type=F32)
            by = lax.dot_general(
                grow2[u], spread[:, at(q * quarter + j * block - g * gw, block)], (((0,), (0,)), ((), ())),
                preferred_element_type=F32,
            )
            out_ref[rows, lanes] = (diag[rows, lanes] + by * carried).astype(BF16)

    def wait_b(messages):
        for m in messages:
            for move in moves_b[m]:
                move.wait_recv()

    def reduce_front(k, p):
        local_state(k, order[2 * p])
        stage_local(k, p)

    own_first = n_head == 2 and n_msg == 4
    own_b.wait()
    loads[3].wait()
    for q in order:
        scale_inputs(own_k, q)
    if own_first:
        reduce_front(own_k, 0)
    pl.semaphore_wait(barrier, expected)
    if not own_first:
        for m in sum(moves_b, []):
            m.start()
        wait_b(range(n_msg))
        reduce_front(own_k, 0)
    move1d.start()
    move1(own_k, 0).start()
    for m in (sum(moves_b, []) if own_first else []) + moves_c:
        m.start()
    local_state(own_k, order[1])
    reduce_front(own_k, 1)
    move1(own_k, 1).start()
    move1d.wait_recv()
    dec2[...] = dec1[...] + decr1[...]
    move2d.start()
    chip_total(own_k, 0)
    local_state(own_k, order[3])
    chip_total(own_k, 1)
    loads[4].wait()
    for q in order:
        scale_inputs(other_k, q)
    own_c.wait()
    before = units // 4 + units // 8
    marks = [before + (i + 1) // 2 * (units // 8) for i in range(n_chunk)] + [before + n_chunk // 2 * (units // 8)]
    if own_first:
        diagonals(0, units // 4)
    move2d.wait_recv()
    pl.when(z == depth - 1)(plane_logs)
    if own_first:
        wait_b((0, 1))
    reduce_front(other_k, 0)
    move1(other_k, 0).start()
    local_state(other_k, order[1])
    chip_total(other_k, 0)
    if own_first:
        wait_b((2, 3))
    reduce_front(other_k, 1)
    move1(other_k, 1).start()
    local_state(other_k, order[3])
    chip_total(other_k, 1)
    pl.when(z == depth - 2)(plane_logs)
    if own_first:
        diagonals(units // 4, before)
    lax.fori_loop(0, n_chunk, lambda i, carry: (slab_chunk(own_k, i), carry)[1], 0)
    pl.when(z == depth - 3)(plane_logs)
    at_end = jnp.logical_or(z == 0, z == depth - 1)
    first = (2 * z) // depth
    last = 1 - first
    if not own_first:
        for m in moves_c:
            m.wait_recv()
        diagonals(0, before)
    for i in range(n_chunk):
        slab_chunk(other_k, i)

        @pl.when(at_end)
        def _():
            chain_step(first, i)

        if own_first and marks[i] <= groups < marks[i + 1]:
            for m in moves_c:
                m.wait_recv()
        diagonals(marks[i], marks[i + 1])
    pl.when(z < depth - 3)(plane_logs)

    done = marks[n_chunk]
    early = min(n_chunk // 2, units - done)

    @pl.when(jnp.logical_not(at_end))
    def _():
        def one(i, carry):
            chain_step(first, i)
            diagonals(done + jnp.minimum(i, early), done + jnp.minimum(i + 1, early))
            return carry

        lax.fori_loop(0, n_chunk, one, 0)

    move5(first, "mine").start()
    pl.when(at_end)(lambda: diagonals(done, units))
    pl.when(at_end)(lambda: expand_other(first))

    @pl.when(z == 0)
    def _():
        for p in ["mine", *range(n_chunk)]:
            move5(0, p).wait_recv()
        lax.fori_loop(0, 4, lambda q, carry: (finish(0, q, range(blocks)), carry)[1], 0)

    for m in sum(moves_b, []) + moves_c + [move1d, move2d]:
        m.wait_send()
    pl.when(z > 0)(move_la.wait_send)
    for k in range(2):
        for p in range(2):
            move1(k, p).wait_send()
        for i in range(n_chunk):
            move2(k, i).wait_send()

    def last_step(i, carry):
        chain_step(last, i)
        pl.when(jnp.logical_and(i == n_chunk // 4, jnp.logical_not(at_end)))(lambda: diagonals(done + early, units))
        return carry

    lax.fori_loop(0, n_chunk, last_step, 0)
    move5(last, "mine").start()
    pl.when(jnp.logical_not(at_end))(lambda: expand_other(first))

    @pl.when(z > 0)
    def _():
        for p in ["mine", *range(n_chunk)]:
            move5(first, p).wait_recv()

    def leave(q, part):
        leaf(q, part)
        pl.when(z > 0)(lambda: finish(0, q, part))
        finish(1, q, part)

    leave(order[3], range(blocks))
    move5(last, "mine").wait_recv()
    leave(order[2], range(blocks))
    step = blocks // n_chunk

    def leave_received(i):
        move5(last, i).wait_recv()
        leave(order[0], range(i * step, (i + 1) * step))

    for i in range(n_chunk):
        expand_chunk(last, i)
        leave(order[1], range(i * step, (i + 1) * step))
        if i > 0:
            leave_received(i - 1)
    leave_received(n_chunk - 1)

    for k in range(2):
        for p in ["mine", *range(n_chunk)]:
            move5(k, p).wait_send()
        for i in range(n_chunk):
            move4(k, i).wait_send()
            pl.when(chain_target(k))(hop(k, i).wait_send)


def shards(n_ctx, n_head, token_values, step_sizes, log_rates, state_write, state_read, skip_gain):
    rows, width = token_values.shape
    heads = width // HEAD_DIM
    groups = state_write.shape[1] // STATE_SIZE // n_head
    per = heads // groups
    half, quarter = width // 2, width // 4
    chunk = min(256, quarter)
    n_chunk = quarter // chunk
    vm = pltpu.VMEM
    dma = pltpu.SemaphoreType.DMA
    n = STATE_SIZE
    scratch = [
        vm((rows, width), BF16), vm(step_sizes.shape, BF16), vm((1, heads), F32), vm((1, heads), F32),
        vm((rows, groups * n), BF16), vm((rows, groups * n), BF16), vm((2 * per, per * HEAD_DIM), BF16),
        vm((2 * groups, per, SPAN), F32), vm((2 * groups, per, SPAN), F32), vm((2 * groups, SPAN, per), F32),
        vm((2 * groups, 2 * per, SPAN), BF16), vm((2 * groups, 2 * per, SPAN), BF16), vm((groups, 8, per), F32),
        vm((rows, width), BF16), vm((2, n, width), F32), vm((rows, width), F32),
        vm((2, 1, width), F32), vm((2, 1, width), F32), vm((2, 1, width), F32), vm((2, 1, width), F32),
        vm((1, width), F32), vm((1, width), F32), vm((3, 1, width), F32),
        vm((2, n, half), BF16), vm((2, n, half), BF16), vm((2, n, quarter), F32),
        vm((2, n, quarter), BF16), vm((2, n, quarter), BF16), vm((2, n, quarter), F32),
        vm((2, n, quarter), BF16), vm((2, n, quarter), BF16), vm((2, n, quarter), BF16), vm((2, n, quarter), BF16),
        vm((2, n, half), BF16), vm((2, n, width), BF16),
        dma((n_head, 4)), dma((n_head, 4)), dma((n_head,)), dma((n_head,)), dma((7,)),
        dma((2, 2)), dma((2, 2)), dma(()), dma(()),
        dma((2, n_chunk)), dma((2, n_chunk)), dma(()), dma(()),
        dma((2, n_chunk)), dma((2, n_chunk)), dma(()), dma(()),
        dma((2, n_chunk)), dma((2, n_chunk)), dma((2, n_chunk + 1)), dma((2, n_chunk + 1)),
    ]
    return pl.pallas_call(
        functools.partial(mixer_kernel, (n_ctx, n_head, heads, groups, chunk)),
        out_shape=jax.ShapeDtypeStruct((rows, width), BF16),
        in_specs=[pl.BlockSpec(memory_space=pltpu.HBM)] * 6,
        out_specs=pl.BlockSpec(memory_space=pltpu.VMEM),
        scratch_shapes=scratch,
        compiler_params=pltpu.CompilerParams(
            collective_id=0, has_side_effects=True, vmem_limit_bytes=45 * 1024 * 1024
        ),
    )(
        *(
            pltpu.with_memory_space_constraint(a, pltpu.HBM)
            for a in (token_values, step_sizes, log_rates[None], state_write, state_read, skip_gain[None])
        )
    )


def solution(mesh):
    placed = (
        P("ctx", "head"),
        P("head", "ctx"),
        P("head"),
        P(("ctx", "head"), None),
        P(("ctx", "head"), None),
        P("head"),
    )
    body = functools.partial(shards, mesh.shape["ctx"], mesh.shape["head"])
    return jax.shard_map(body, mesh=mesh, in_specs=placed, out_specs=P("ctx", "head"), check_vma=False)
```
